1024 devices in a mesh: row: 32 (over z_lo, x, core), col: 32 (over z_hi, y).
Axes of the slice: x: 4, y: 8, z: 16 (z_hi: 4, z_lo: 4; z = z_hi * 4 + z_lo), core: 2. Of those that a mesh axis runs over, the one named last changes fastest.
Arguments:
- obj: float32 [2, 2, 4096, 4096], P(None, None, 'row', 'col'), may hold values from -4 to 4
- bank: bfloat16 [8, 2, 128, 128], replicated, may hold values from -0.21875 to 0.21875
- band_index: int32 [2, 2, 3], replicated, may hold values from 0 to 7
- tilt: int32 [2, 2], replicated, may hold values from -24 to 23
- tile_shift: int32 [2, 2], replicated, may hold values from 0 to 7
- slice_order: int32 [2], replicated, may hold values from 0 to 1, each once
- cot: bfloat16 [2, 2, 4096, 4096], P(None, None, 'row', 'col'), may hold values from -6 to 6
Outputs:
- exit_field: bfloat16 [2, 2, 4096, 4096], P(None, None, 'row', 'col')
- grad_obj: float32 [2, 2, 4096, 4096], P(None, None, 'row', 'col')
The draws below stay inside these ranges and needn't reach their ends.
All inputs are finite; a program needn't handle non-finite values.
Results may differ from the reference program's by a relative error of at most 0.014.
Values may be sent and summed in bfloat16 or wider, within the bound.
A program may use at most 32 MiB of HBM per device.

```python
import math
import jax
import jax.numpy as jnp
from jax import lax

BLK = 128
NBANK = 8
SL = 2
ANG = 2
TR = 128
TC = 128
NR = 4096
NC = 4096
SHIFT = 8


def touch_ends(values, own_key, smallest, high):
    longest = values.shape.index(max(values.shape))
    spots = []
    for shift in (0, 1):
        where = [jax.random.randint(jax.random.fold_in(own_key, axis), (), 0, length) for axis, length in enumerate(values.shape)]
        where[longest] = (where[longest] + shift) % values.shape[longest]
        spots.append(tuple(where))
    return values.at[spots[0]].set(smallest).at[spots[1]].set(high)


def block_scale(own_key, dims, pieces, low, largest):
    factor_of = 1.0
    for dim, parts in pieces:
        heights = jax.random.uniform(jax.random.fold_in(jax.random.fold_in(own_key, 6), dim), (parts,), jnp.float32, low / len(pieces), largest / len(pieces))
        factor_of = factor_of * jnp.repeat(jnp.exp(heights), dims[dim] // parts).reshape((-1,) + (1,) * (len(dims) - 1 - dim))
    return factor_of


def centred(own_key, extent, deviation, most, shards=(), kind=jnp.bfloat16):
    drawn = jax.random.normal(own_key, extent, jnp.float32) * deviation
    if len(shards) > 0:
        drawn = block_scale(own_key, extent, shards, -0.22, 0.18) * drawn
    return jnp.clip(drawn, min=-most, max=most).astype(kind)


def setup_inputs(seed: int = 0) -> dict:
    splits = jax.random.split(jax.random.key(seed), 8)
    return {
        "obj": centred(splits[0], (SL, 2, NR, NC), 0.7, 4.0, ((2, 32), (3, 32)), jnp.float32),
        "bank": centred(splits[1], (NBANK, 2, BLK, BLK), (6 * BLK) ** -0.5, 0.21875),
        "band_index": touch_ends(jax.random.randint(splits[2], (SL, 2, 3), 0, NBANK), jax.random.fold_in(splits[2], 1), 0, NBANK - 1).astype(jnp.int32),
        "tilt": touch_ends(jax.random.randint(splits[3], (ANG, 2), -24, 24), jax.random.fold_in(splits[3], 1), -24, 23).astype(jnp.int32),
        "tile_shift": touch_ends(jax.random.randint(splits[4], (ANG, 2), 0, SHIFT), jax.random.fold_in(splits[4], 1), 0, SHIFT - 1).astype(jnp.int32),
        "slice_order": jax.random.permutation(splits[5], SL).astype(jnp.int32),
        "cot": centred(splits[6], (ANG, 2, NR, NC), 1.0, 6.0, ((2, 32), (3, 32))),
    }


def incident(tilt_row, tilt_col, row_start, col_start, rows, cols, total_rows, total_cols):
    row_ids = row_start + jnp.arange(rows, dtype=jnp.int32)
    col_ids = col_start + jnp.arange(cols, dtype=jnp.int32)
    row_phase = jnp.mod(tilt_row * row_ids, total_rows).astype(jnp.float32) / total_rows
    col_phase = jnp.mod(tilt_col * col_ids, total_cols).astype(jnp.float32) / total_cols
    phase = (2.0 * math.pi) * (row_phase[:, None] + col_phase[None, :])
    return jnp.stack([jnp.cos(phase), jnp.sin(phase)]).astype(jnp.bfloat16)


def wrap_pad(field, width, axis):
    length = field.shape[axis]
    lower = lax.slice_in_dim(field, length - width, length, axis=axis)
    upper = lax.slice_in_dim(field, 0, width, axis=axis)
    return jnp.concatenate([lower, field, upper], axis=axis)


def rows_product(matrix, field, width, adjoint):
    lead, rows, cols = field.shape
    blocks = field.reshape(lead, rows // width, width, cols)
    form = "qp,anqc->anpc" if adjoint else "pq,anqc->anpc"
    return jnp.einsum(form, matrix, blocks, precision=lax.Precision.HIGHEST).reshape(lead, rows, cols)


def cols_product(matrix, field, width, adjoint):
    lead, rows, cols = field.shape
    blocks = field.reshape(lead, rows, cols // width, width)
    form = "arnq,pq->arnp" if adjoint else "arnq,qp->arnp"
    return jnp.einsum(form, blocks, matrix, precision=lax.Precision.HIGHEST).reshape(lead, rows, cols)


def band_apply(padded, mats, length, axis, adjoint):
    width = mats[0][0].shape[0]
    total_real = None
    total_imag = None
    for position in range(3):
        offset = position - 1
        start = width * (1 - offset) if adjoint else width * (1 + offset)
        segment = lax.slice_in_dim(padded, start, start + length, axis=axis).astype(jnp.float32)
        real_in = segment[:, 0]
        imag_in = segment[:, 1]
        mat_real = mats[position][0].astype(jnp.float32)
        mat_imag = mats[position][1].astype(jnp.float32)
        if axis == 2:
            product = rows_product
        else:
            product = cols_product
        if adjoint:
            part_real = product(mat_real, real_in, width, True) + product(mat_imag, imag_in, width, True)
            part_imag = product(mat_real, imag_in, width, True) - product(mat_imag, real_in, width, True)
        else:
            part_real = product(mat_real, real_in, width, False) - product(mat_imag, imag_in, width, False)
            part_imag = product(mat_real, imag_in, width, False) + product(mat_imag, real_in, width, False)
        total_real = part_real if total_real is None else total_real + part_real
        total_imag = part_imag if total_imag is None else total_imag + part_imag
    return jnp.stack([total_real, total_imag], axis=1).astype(jnp.bfloat16)


def transmit(trans, field):
    field_real = field[:, 0].astype(jnp.float32)
    field_imag = field[:, 1].astype(jnp.float32)
    out_real = trans[0] * field_real - trans[1] * field_imag
    out_imag = trans[0] * field_imag + trans[1] * field_real
    return jnp.stack([out_real, out_imag], axis=1).astype(jnp.bfloat16)


def reference(obj, bank, band_index, tilt, tile_shift, slice_order, cot):
    width = bank.shape[2]
    grad = jnp.zeros(obj.shape, jnp.float32)
    exits = []
    for angle in range(ANG):
        field = incident(tilt[angle, 0], tilt[angle, 1], 0, 0, NR, NC, NR, NC)[None]
        saved = []
        for layer in range(SL):
            saved.append(field)
            trans = obj[slice_order[layer]]
            field = transmit(trans, field)
            row_mats = [(bank[band_index[layer, 0, p], 0], bank[band_index[layer, 0, p], 1]) for p in range(3)]
            col_mats = [(bank[band_index[layer, 1, p], 0], bank[band_index[layer, 1, p], 1]) for p in range(3)]
            field = band_apply(wrap_pad(field, width, 2), row_mats, NR, 2, False)
            field = band_apply(wrap_pad(field, width, 3), col_mats, NC, 3, False)
        exits.append(jnp.roll(field[0], (tile_shift[angle, 0] * TR, tile_shift[angle, 1] * TC), axis=(1, 2)))
        grad_field = jnp.roll(cot[angle], (-tile_shift[angle, 0] * TR, -tile_shift[angle, 1] * TC), axis=(1, 2))[None]
        for layer in range(SL - 1, -1, -1):
            row_mats = [(bank[band_index[layer, 0, p], 0], bank[band_index[layer, 0, p], 1]) for p in range(3)]
            col_mats = [(bank[band_index[layer, 1, p], 0], bank[band_index[layer, 1, p], 1]) for p in range(3)]
            back_cols = band_apply(wrap_pad(grad_field, width, 3), col_mats, NC, 3, True)
            back_rows = band_apply(wrap_pad(back_cols, width, 2), row_mats, NR, 2, True)
            grad_real = back_rows[0, 0].astype(jnp.float32)
            grad_imag = back_rows[0, 1].astype(jnp.float32)
            psi_real = saved[layer][0, 0].astype(jnp.float32)
            psi_imag = saved[layer][0, 1].astype(jnp.float32)
            term = jnp.stack([grad_real * psi_real + grad_imag * psi_imag, grad_imag * psi_real - grad_real * psi_imag])
            grad = grad.at[slice_order[layer]].add(term)
            if layer > 0:
                trans = obj[slice_order[layer]]
                grad_field = jnp.stack([grad_real * trans[0] + grad_imag * trans[1], grad_imag * trans[0] - grad_real * trans[1]])[None].astype(jnp.bfloat16)
    return jnp.stack(exits), grad
```

```python
import functools
import math

import jax
import jax.numpy as jnp
from jax import lax
from jax.experimental import pallas as pl
from jax.experimental.pallas import tpu as pltpu
from jax.sharding import PartitionSpec as P

MESH = pl.DeviceIdType.MESH
SHIFTS = 8


def left_matrix(bank, index):
    real, imag = bank[index, 0], bank[index, 1]
    return jnp.concatenate(
        [jnp.concatenate([real, -imag], axis=1), jnp.concatenate([imag, real], axis=1)], axis=0
    )


def left_adjoint(bank, index):
    real = bank[index, 0].astype(jnp.float32).T.astype(jnp.bfloat16)
    imag = bank[index, 1].astype(jnp.float32).T.astype(jnp.bfloat16)
    return jnp.concatenate(
        [jnp.concatenate([real, imag], axis=1), jnp.concatenate([-imag, real], axis=1)], axis=0
    )


def right_matrix(bank, index):
    real, imag = bank[index, 0], bank[index, 1]
    return jnp.concatenate(
        [jnp.concatenate([real, imag], axis=1), jnp.concatenate([-imag, real], axis=1)], axis=0
    )


def by_component(ref):
    return jnp.concatenate(
        [
            jnp.concatenate([ref[0, 0], ref[1, 0]], axis=1),
            jnp.concatenate([ref[0, 1], ref[1, 1]], axis=1),
        ],
        axis=0,
    )


def by_angle(ref):
    return jnp.concatenate(
        [
            jnp.concatenate([ref[0, 0], ref[0, 1]], axis=1),
            jnp.concatenate([ref[1, 0], ref[1, 1]], axis=1),
        ],
        axis=0,
    )


def row_term(matrix, ref):
    return jnp.dot(matrix, by_component(ref), preferred_element_type=jnp.float32)


def col_term(ref, matrix):
    return jnp.dot(by_angle(ref), matrix, preferred_element_type=jnp.float32)


def col_adjoint_term(ref, matrix):
    return lax.dot_general(
        by_angle(ref), matrix, (((1,), (1,)), ((), ())), preferred_element_type=jnp.float32
    )


def from_component(total, angle, part):
    n = total.shape[0] // 2
    return total[part * n : (part + 1) * n, angle * n : (angle + 1) * n]


def from_angle(total, angle, part):
    n = total.shape[0] // 2
    return total[angle * n : (angle + 1) * n, part * n : (part + 1) * n]


def incident(tilt, row_start, col_start, period, width):
    line = lax.broadcasted_iota(jnp.int32, (8, width), 0)
    spot = lax.broadcasted_iota(jnp.int32, (8, width), 1)
    rate = jnp.where(
        line == 0,
        tilt[0, 0],
        jnp.where(line == 1, tilt[0, 1], jnp.where(line == 2, tilt[1, 0], tilt[1, 1])),
    )
    start = jnp.where(line % 2 == 0, row_start, col_start)
    turns = (rate * (start + spot)) & (period - 1)
    phase = turns.astype(jnp.float32) * (2.0 * math.pi / period)
    cos, sin = jnp.cos(phase), jnp.sin(phase)
    cos_t, sin_t = cos.T, sin.T
    fields = []
    for angle in range(2):
        row_cos = cos_t[:, 2 * angle : 2 * angle + 1]
        row_sin = sin_t[:, 2 * angle : 2 * angle + 1]
        col_cos = cos[2 * angle + 1 : 2 * angle + 2, :]
        col_sin = sin[2 * angle + 1 : 2 * angle + 2, :]
        fields.append(
            (
                (row_cos * col_cos - row_sin * col_sin).astype(jnp.bfloat16),
                (row_sin * col_cos + row_cos * col_sin).astype(jnp.bfloat16),
            )
        )
    return fields


class Halo:
    def __init__(self, axis, count, source, low, high, sems, slot):
        here = lax.axis_index(axis)
        after = lax.rem(here + 1, count)
        before = lax.rem(here + count - 1, count)
        send, recv = sems
        self.up = pltpu.make_async_remote_copy(
            src_ref=source,
            dst_ref=low,
            send_sem=send.at[slot],
            recv_sem=recv.at[slot],
            device_id={axis: after},
            device_id_type=MESH,
        )
        self.down = pltpu.make_async_remote_copy(
            src_ref=source,
            dst_ref=high,
            send_sem=send.at[slot + 1],
            recv_sem=recv.at[slot + 1],
            device_id={axis: before},
            device_id_type=MESH,
        )

    def start(self):
        self.up.start()
        self.down.start()

    def wait_send(self):
        self.up.wait_send()
        self.down.wait_send()


def greet(axes):
    barrier = pltpu.get_barrier_semaphore()
    for axis, count in axes:
        here = lax.axis_index(axis)
        for other in (lax.rem(here + 1, count), lax.rem(here + count - 1, count)):
            pl.semaphore_signal(barrier, inc=1, device_id={axis: other}, device_id_type=MESH)


def met(number):
    pl.semaphore_wait(pltpu.get_barrier_semaphore(), number)


def first(rows, cols, order, band, tilt, obj, bank, cot, u_out, psi_out, q_out, *scratch):
    u_mine, v_mine, h_mine, rim, send, recv = scratch
    width = bank.shape[2]
    greet((("row", rows), ("col", cols)))
    row_start = lax.axis_index("row") * width
    col_start = lax.axis_index("col") * width
    here, later = order[0], order[1]
    fields = incident(tilt, row_start, col_start, rows * width, width)
    t_real, t_imag = obj[here, 0], obj[here, 1]
    for angle in range(2):
        real = fields[angle][0].astype(jnp.float32)
        imag = fields[angle][1].astype(jnp.float32)
        u_mine[angle, 0] = (t_real * real - t_imag * imag).astype(jnp.bfloat16)
        u_mine[angle, 1] = (t_real * imag + t_imag * real).astype(jnp.bfloat16)
    met(4)
    sems = (send, recv)
    halo_u = Halo("row", rows, u_mine, rim.at[0], rim.at[1], sems, 0)
    halo_g = Halo("col", cols, cot, rim.at[2], rim.at[3], sems, 2)
    halo_v = Halo("col", cols, v_mine, rim.at[4], rim.at[5], sems, 4)
    halo_h = Halo("row", rows, h_mine, rim.at[6], rim.at[7], sems, 6)
    halo_g.start()
    halo_u.start()
    v = row_term(left_matrix(bank, band[0, 0, 1]), u_mine)
    h = col_adjoint_term(cot, right_matrix(bank, band[1, 1, 1]))
    halo_u.up.wait_recv()
    v += row_term(left_matrix(bank, band[0, 0, 0]), rim.at[0])
    halo_u.down.wait_recv()
    v += row_term(left_matrix(bank, band[0, 0, 2]), rim.at[1])
    for angle in range(2):
        for part in range(2):
            v_mine[angle, part] = from_component(v, angle, part).astype(jnp.bfloat16)
    halo_v.start()
    halo_g.up.wait_recv()
    h += col_adjoint_term(rim.at[2], right_matrix(bank, band[1, 1, 2]))
    halo_g.down.wait_recv()
    h += col_adjoint_term(rim.at[3], right_matrix(bank, band[1, 1, 0]))
    for angle in range(2):
        for part in range(2):
            h_mine[angle, part] = from_angle(h, angle, part).astype(jnp.bfloat16)
    halo_h.start()
    q = row_term(left_adjoint(bank, band[1, 0, 1]), h_mine)
    p = col_term(v_mine, right_matrix(bank, band[0, 1, 1]))
    halo_h.up.wait_recv()
    q += row_term(left_adjoint(bank, band[1, 0, 2]), rim.at[6])
    halo_h.down.wait_recv()
    q += row_term(left_adjoint(bank, band[1, 0, 0]), rim.at[7])
    for angle in range(2):
        for part in range(2):
            q_out[angle, part] = from_component(q, angle, part).astype(jnp.bfloat16)
    halo_v.up.wait_recv()
    p += col_term(rim.at[4], right_matrix(bank, band[0, 1, 0]))
    halo_v.down.wait_recv()
    p += col_term(rim.at[5], right_matrix(bank, band[0, 1, 2]))
    s_real, s_imag = obj[later, 0], obj[later, 1]
    for angle in range(2):
        real = from_angle(p, angle, 0).astype(jnp.bfloat16)
        imag = from_angle(p, angle, 1).astype(jnp.bfloat16)
        psi_out[angle, 0] = real
        psi_out[angle, 1] = imag
        real, imag = real.astype(jnp.float32), imag.astype(jnp.float32)
        u_out[angle, 0] = (s_real * real - s_imag * imag).astype(jnp.bfloat16)
        u_out[angle, 1] = (s_real * imag + s_imag * real).astype(jnp.bfloat16)
    for halo in (halo_u, halo_g, halo_v, halo_h):
        halo.wait_send()


def second(rows, cols, order, band, tilt, obj, bank, u, q, psi, exit_out, grad_out, *scratch):
    g_mine, v_mine, h_mine, rim, send, recv = scratch
    width = bank.shape[2]
    greet((("row", rows), ("col", cols)))
    row_start = lax.axis_index("row") * width
    col_start = lax.axis_index("col") * width
    later = order[1]
    s_real, s_imag = obj[later, 0], obj[later, 1]
    last_real = None
    last_imag = None
    for angle in range(2):
        q_real, q_imag = q[angle, 0].astype(jnp.float32), q[angle, 1].astype(jnp.float32)
        g_mine[angle, 0] = (q_real * s_real + q_imag * s_imag).astype(jnp.bfloat16)
        g_mine[angle, 1] = (q_imag * s_real - q_real * s_imag).astype(jnp.bfloat16)
        real, imag = psi[angle, 0].astype(jnp.float32), psi[angle, 1].astype(jnp.float32)
        add_real = q_real * real + q_imag * imag
        add_imag = q_imag * real - q_real * imag
        last_real = add_real if last_real is None else last_real + add_real
        last_imag = add_imag if last_imag is None else last_imag + add_imag
    met(4)
    sems = (send, recv)
    halo_u = Halo("row", rows, u, rim.at[0], rim.at[1], sems, 0)
    halo_g = Halo("col", cols, g_mine, rim.at[2], rim.at[3], sems, 2)
    halo_v = Halo("col", cols, v_mine, rim.at[4], rim.at[5], sems, 4)
    halo_h = Halo("row", rows, h_mine, rim.at[6], rim.at[7], sems, 6)
    halo_g.start()
    halo_u.start()
    v = row_term(left_matrix(bank, band[1, 0, 1]), u)
    h = col_adjoint_term(g_mine, right_matrix(bank, band[0, 1, 1]))
    halo_u.up.wait_recv()
    v += row_term(left_matrix(bank, band[1, 0, 0]), rim.at[0])
    halo_u.down.wait_recv()
    v += row_term(left_matrix(bank, band[1, 0, 2]), rim.at[1])
    for angle in range(2):
        for part in range(2):
            v_mine[angle, part] = from_component(v, angle, part).astype(jnp.bfloat16)
    halo_v.start()
    halo_g.up.wait_recv()
    h += col_adjoint_term(rim.at[2], right_matrix(bank, band[0, 1, 2]))
    halo_g.down.wait_recv()
    h += col_adjoint_term(rim.at[3], right_matrix(bank, band[0, 1, 0]))
    for angle in range(2):
        for part in range(2):
            h_mine[angle, part] = from_angle(h, angle, part).astype(jnp.bfloat16)
    halo_h.start()
    fields = incident(tilt, row_start, col_start, rows * width, width)
    b = row_term(left_adjoint(bank, band[0, 0, 1]), h_mine)
    p = col_term(v_mine, right_matrix(bank, band[1, 1, 1]))
    halo_h.up.wait_recv()
    b += row_term(left_adjoint(bank, band[0, 0, 2]), rim.at[6])
    halo_h.down.wait_recv()
    b += row_term(left_adjoint(bank, band[0, 0, 0]), rim.at[7])
    first_real = None
    first_imag = None
    for angle in range(2):
        q_real = from_component(b, angle, 0).astype(jnp.bfloat16).astype(jnp.float32)
        q_imag = from_component(b, angle, 1).astype(jnp.bfloat16).astype(jnp.float32)
        real, imag = fields[angle][0].astype(jnp.float32), fields[angle][1].astype(jnp.float32)
        add_real = q_real * real + q_imag * imag
        add_imag = q_imag * real - q_real * imag
        first_real = add_real if first_real is None else first_real + add_real
        first_imag = add_imag if first_imag is None else first_imag + add_imag
    swapped = later == 0
    grad_out[0, 0] = jnp.where(swapped, last_real, first_real)
    grad_out[0, 1] = jnp.where(swapped, last_imag, first_imag)
    grad_out[1, 0] = jnp.where(swapped, first_real, last_real)
    grad_out[1, 1] = jnp.where(swapped, first_imag, last_imag)
    halo_v.up.wait_recv()
    p += col_term(rim.at[4], right_matrix(bank, band[1, 1, 0]))
    halo_v.down.wait_recv()
    p += col_term(rim.at[5], right_matrix(bank, band[1, 1, 2]))
    for angle in range(2):
        for part in range(2):
            exit_out[angle, part] = from_angle(p, angle, part).astype(jnp.bfloat16)
    for halo in (halo_u, halo_g, halo_v, halo_h):
        halo.wait_send()


def call(body, outs, arrays, width, number):
    field = (2, 2, width, width)
    smem = pl.BlockSpec(memory_space=pltpu.SMEM)
    vmem = pl.BlockSpec(memory_space=pltpu.VMEM)
    return pl.pallas_call(
        body,
        out_shape=outs,
        in_specs=[smem] * 3 + [vmem] * (len(arrays) - 3),
        out_specs=[vmem] * len(outs),
        scratch_shapes=[
            pltpu.VMEM(field, jnp.bfloat16),
            pltpu.VMEM(field, jnp.bfloat16),
            pltpu.VMEM(field, jnp.bfloat16),
            pltpu.VMEM((8, *field), jnp.bfloat16),
            pltpu.SemaphoreType.DMA((8,)),
            pltpu.SemaphoreType.DMA((8,)),
        ],
        compiler_params=pltpu.CompilerParams(collective_id=number, has_side_effects=True),
    )(*arrays)


def move(row_step, col_step, rows, cols, u, q):
    if row_step == 0 and col_step == 0:
        return u, q
    there = []
    for row in range(rows):
        for col in range(cols):
            target = (row + row_step) % rows * cols + (col + col_step) % cols
            there.append((row * cols + col, target))
    back = [(target, source) for source, target in there]
    axes = ("row", "col")
    return lax.ppermute(u, axes, there), lax.ppermute(q, axes, back)


def local(rows, cols, obj, bank, band_index, tilt, tile_shift, slice_order, cot):
    width = bank.shape[2]
    small = jax.ShapeDtypeStruct(cot.shape, jnp.bfloat16)
    u, psi, q = call(
        functools.partial(first, rows, cols),
        (small, small, small),
        (slice_order, band_index, tilt, obj, bank, cot),
        width,
        0,
    )
    choice = tile_shift[:, 0] * SHIFTS + tile_shift[:, 1]
    branches = [
        functools.partial(move, row_step, col_step, rows, cols)
        for row_step in range(SHIFTS)
        for col_step in range(SHIFTS)
    ]
    moved = [lax.switch(choice[angle], branches, u[angle], q[angle]) for angle in range(2)]
    u = jnp.stack([moved[0][0], moved[1][0]])
    q = jnp.stack([moved[0][1], moved[1][1]])
    exit_field, grad = call(
        functools.partial(second, rows, cols),
        (small, jax.ShapeDtypeStruct(obj.shape, jnp.float32)),
        (slice_order, band_index, tilt, obj, bank, u, q, psi),
        width,
        1,
    )
    return exit_field, grad


def solution(mesh):
    field = P(None, None, "row", "col")
    return jax.shard_map(
        functools.partial(local, mesh.shape["row"], mesh.shape["col"]),
        mesh=mesh,
        in_specs=(field, P(), P(), P(), P(), P(), field),
        out_specs=(field, field),
        check_vma=False,
    )
```

```python
import functools
import math

import jax
import jax.numpy as jnp
from jax import lax
from jax.experimental import pallas as pl
from jax.experimental.pallas import tpu as pltpu
from jax.sharding import PartitionSpec as P

MESH = pl.DeviceIdType.MESH
SHIFTS = 8
VMEM_LIMIT = 16 << 20


def left_matrix(bank, index):
    real, imag = bank[index, 0], bank[index, 1]
    return jnp.concatenate(
        [jnp.concatenate([real, -imag], axis=1), jnp.concatenate([imag, real], axis=1)], axis=0
    )


def left_adjoint(bank, index):
    real = bank[index, 0].astype(jnp.float32).T.astype(jnp.bfloat16)
    imag = bank[index, 1].astype(jnp.float32).T.astype(jnp.bfloat16)
    return jnp.concatenate(
        [jnp.concatenate([real, imag], axis=1), jnp.concatenate([-imag, real], axis=1)], axis=0
    )


def right_matrix(bank, index):
    real, imag = bank[index, 0], bank[index, 1]
    return jnp.concatenate(
        [jnp.concatenate([real, imag], axis=1), jnp.concatenate([-imag, real], axis=1)], axis=0
    )


def by_component(ref):
    return jnp.concatenate(
        [
            jnp.concatenate([ref[0, 0], ref[1, 0]], axis=1),
            jnp.concatenate([ref[0, 1], ref[1, 1]], axis=1),
        ],
        axis=0,
    )


def by_angle(ref):
    return jnp.concatenate(
        [
            jnp.concatenate([ref[0, 0], ref[0, 1]], axis=1),
            jnp.concatenate([ref[1, 0], ref[1, 1]], axis=1),
        ],
        axis=0,
    )


def row_term(matrix, ref):
    return jnp.dot(matrix, by_component(ref), preferred_element_type=jnp.float32)


def col_term(ref, matrix):
    return jnp.dot(by_angle(ref), matrix, preferred_element_type=jnp.float32)


def col_adjoint_term(ref, matrix):
    return lax.dot_general(
        by_angle(ref), matrix, (((1,), (1,)), ((), ())), preferred_element_type=jnp.float32
    )


def from_component(total, angle, part):
    n = total.shape[0] // 2
    return total[part * n : (part + 1) * n, angle * n : (angle + 1) * n]


def from_angle(total, angle, part):
    n = total.shape[0] // 2
    return total[angle * n : (angle + 1) * n, part * n : (part + 1) * n]


def incident(tilt, row_start, col_start, period, width):
    line = lax.broadcasted_iota(jnp.int32, (8, width), 0)
    spot = lax.broadcasted_iota(jnp.int32, (8, width), 1)
    rate = jnp.where(
        line == 0,
        tilt[0, 0],
        jnp.where(line == 1, tilt[0, 1], jnp.where(line == 2, tilt[1, 0], tilt[1, 1])),
    )
    start = jnp.where(line % 2 == 0, row_start, col_start)
    turns = (rate * (start + spot)) & (period - 1)
    phase = turns.astype(jnp.float32) * (2.0 * math.pi / period)
    cos, sin = jnp.cos(phase), jnp.sin(phase)
    cos_t, sin_t = cos.T, sin.T
    fields = []
    for angle in range(2):
        row_cos = cos_t[:, 2 * angle : 2 * angle + 1]
        row_sin = sin_t[:, 2 * angle : 2 * angle + 1]
        col_cos = cos[2 * angle + 1 : 2 * angle + 2, :]
        col_sin = sin[2 * angle + 1 : 2 * angle + 2, :]
        fields.append(
            (
                (row_cos * col_cos - row_sin * col_sin).astype(jnp.bfloat16),
                (row_sin * col_cos + row_cos * col_sin).astype(jnp.bfloat16),
            )
        )
    return fields


class Halo:
    def __init__(self, axis, count, source, low, high, sems, slot):
        here = lax.axis_index(axis)
        after = lax.rem(here + 1, count)
        before = lax.rem(here + count - 1, count)
        send, recv = sems
        self.up = pltpu.make_async_remote_copy(
            src_ref=source,
            dst_ref=low,
            send_sem=send.at[slot],
            recv_sem=recv.at[slot],
            device_id={axis: after},
            device_id_type=MESH,
        )
        self.down = pltpu.make_async_remote_copy(
            src_ref=source,
            dst_ref=high,
            send_sem=send.at[slot + 1],
            recv_sem=recv.at[slot + 1],
            device_id={axis: before},
            device_id_type=MESH,
        )

    def start(self):
        self.up.start()
        self.down.start()

    def wait_send(self):
        self.up.wait_send()
        self.down.wait_send()


def greet(axes):
    barrier = pltpu.get_barrier_semaphore()
    for axis, count in axes:
        here = lax.axis_index(axis)
        for other in (lax.rem(here + 1, count), lax.rem(here + count - 1, count)):
            pl.semaphore_signal(barrier, inc=1, device_id={axis: other}, device_id_type=MESH)


def met(number):
    pl.semaphore_wait(pltpu.get_barrier_semaphore(), number)


def first(rows, cols, order, band, tilt, obj, bank, cot, u_0, u_1, q_0, q_1, psi_out, *scratch):
    u_out, q_out = (u_0, u_1), (q_0, q_1)
    u_mine, v_mine, h_mine, rim, send, recv = scratch
    width = bank.shape[2]
    greet((("row", rows), ("col", cols)))
    row_start = lax.axis_index("row") * width
    col_start = lax.axis_index("col") * width
    here, later = order[0], order[1]
    fields = incident(tilt, row_start, col_start, rows * width, width)
    t_real, t_imag = obj[here, 0], obj[here, 1]
    for angle in range(2):
        real = fields[angle][0].astype(jnp.float32)
        imag = fields[angle][1].astype(jnp.float32)
        u_mine[angle, 0] = (t_real * real - t_imag * imag).astype(jnp.bfloat16)
        u_mine[angle, 1] = (t_real * imag + t_imag * real).astype(jnp.bfloat16)
    met(4)
    sems = (send, recv)
    halo_u = Halo("row", rows, u_mine, rim.at[0], rim.at[1], sems, 0)
    halo_g = Halo("col", cols, cot, rim.at[2], rim.at[3], sems, 2)
    halo_v = Halo("col", cols, v_mine, rim.at[4], rim.at[5], sems, 4)
    halo_h = Halo("row", rows, h_mine, rim.at[6], rim.at[7], sems, 6)
    halo_g.start()
    halo_u.start()
    v = row_term(left_matrix(bank, band[0, 0, 1]), u_mine)
    h = col_adjoint_term(cot, right_matrix(bank, band[1, 1, 1]))
    halo_u.up.wait_recv()
    v += row_term(left_matrix(bank, band[0, 0, 0]), rim.at[0])
    halo_u.down.wait_recv()
    v += row_term(left_matrix(bank, band[0, 0, 2]), rim.at[1])
    for angle in range(2):
        for part in range(2):
            v_mine[angle, part] = from_component(v, angle, part).astype(jnp.bfloat16)
    halo_v.start()
    halo_g.up.wait_recv()
    h += col_adjoint_term(rim.at[2], right_matrix(bank, band[1, 1, 2]))
    halo_g.down.wait_recv()
    h += col_adjoint_term(rim.at[3], right_matrix(bank, band[1, 1, 0]))
    for angle in range(2):
        for part in range(2):
            h_mine[angle, part] = from_angle(h, angle, part).astype(jnp.bfloat16)
    halo_h.start()
    q = row_term(left_adjoint(bank, band[1, 0, 1]), h_mine)
    p = col_term(v_mine, right_matrix(bank, band[0, 1, 1]))
    halo_h.up.wait_recv()
    q += row_term(left_adjoint(bank, band[1, 0, 2]), rim.at[6])
    halo_h.down.wait_recv()
    q += row_term(left_adjoint(bank, band[1, 0, 0]), rim.at[7])
    for angle in range(2):
        for part in range(2):
            q_out[angle][part] = from_component(q, angle, part).astype(jnp.bfloat16)
    halo_v.up.wait_recv()
    p += col_term(rim.at[4], right_matrix(bank, band[0, 1, 0]))
    halo_v.down.wait_recv()
    p += col_term(rim.at[5], right_matrix(bank, band[0, 1, 2]))
    s_real, s_imag = obj[later, 0], obj[later, 1]
    for angle in range(2):
        real = from_angle(p, angle, 0).astype(jnp.bfloat16)
        imag = from_angle(p, angle, 1).astype(jnp.bfloat16)
        psi_out[angle, 0] = real
        psi_out[angle, 1] = imag
        real, imag = real.astype(jnp.float32), imag.astype(jnp.float32)
        u_out[angle][0] = (s_real * real - s_imag * imag).astype(jnp.bfloat16)
        u_out[angle][1] = (s_real * imag + s_imag * real).astype(jnp.bfloat16)
    for halo in (halo_u, halo_g, halo_v, halo_h):
        halo.wait_send()


def second(rows, cols, order, band, tilt, obj, bank, u_0, u_1, q_0, q_1, psi, exit_out, grad_out, *scratch):
    g_mine, v_mine, h_mine, rim, send, recv, u = scratch
    q = (q_0, q_1)
    u[0] = u_0[...]
    u[1] = u_1[...]
    width = bank.shape[2]
    greet((("row", rows), ("col", cols)))
    row_start = lax.axis_index("row") * width
    col_start = lax.axis_index("col") * width
    later = order[1]
    s_real, s_imag = obj[later, 0], obj[later, 1]
    last_real = None
    last_imag = None
    for angle in range(2):
        q_real, q_imag = q[angle][0].astype(jnp.float32), q[angle][1].astype(jnp.float32)
        g_mine[angle, 0] = (q_real * s_real + q_imag * s_imag).astype(jnp.bfloat16)
        g_mine[angle, 1] = (q_imag * s_real - q_real * s_imag).astype(jnp.bfloat16)
        real, imag = psi[angle, 0].astype(jnp.float32), psi[angle, 1].astype(jnp.float32)
        add_real = q_real * real + q_imag * imag
        add_imag = q_imag * real - q_real * imag
        last_real = add_real if last_real is None else last_real + add_real
        last_imag = add_imag if last_imag is None else last_imag + add_imag
    met(4)
    sems = (send, recv)
    halo_u = Halo("row", rows, u, rim.at[0], rim.at[1], sems, 0)
    halo_g = Halo("col", cols, g_mine, rim.at[2], rim.at[3], sems, 2)
    halo_v = Halo("col", cols, v_mine, rim.at[4], rim.at[5], sems, 4)
    halo_h = Halo("row", rows, h_mine, rim.at[6], rim.at[7], sems, 6)
    halo_g.start()
    halo_u.start()
    v = row_term(left_matrix(bank, band[1, 0, 1]), u)
    h = col_adjoint_term(g_mine, right_matrix(bank, band[0, 1, 1]))
    halo_u.up.wait_recv()
    v += row_term(left_matrix(bank, band[1, 0, 0]), rim.at[0])
    halo_u.down.wait_recv()
    v += row_term(left_matrix(bank, band[1, 0, 2]), rim.at[1])
    for angle in range(2):
        for part in range(2):
            v_mine[angle, part] = from_component(v, angle, part).astype(jnp.bfloat16)
    halo_v.start()
    halo_g.up.wait_recv()
    h += col_adjoint_term(rim.at[2], right_matrix(bank, band[0, 1, 2]))
    halo_g.down.wait_recv()
    h += col_adjoint_term(rim.at[3], right_matrix(bank, band[0, 1, 0]))
    for angle in range(2):
        for part in range(2):
            h_mine[angle, part] = from_angle(h, angle, part).astype(jnp.bfloat16)
    halo_h.start()
    fields = incident(tilt, row_start, col_start, rows * width, width)
    b = row_term(left_adjoint(bank, band[0, 0, 1]), h_mine)
    p = col_term(v_mine, right_matrix(bank, band[1, 1, 1]))
    halo_h.up.wait_recv()
    b += row_term(left_adjoint(bank, band[0, 0, 2]), rim.at[6])
    halo_h.down.wait_recv()
    b += row_term(left_adjoint(bank, band[0, 0, 0]), rim.at[7])
    first_real = None
    first_imag = None
    for angle in range(2):
        q_real = from_component(b, angle, 0).astype(jnp.bfloat16).astype(jnp.float32)
        q_imag = from_component(b, angle, 1).astype(jnp.bfloat16).astype(jnp.float32)
        real, imag = fields[angle][0].astype(jnp.float32), fields[angle][1].astype(jnp.float32)
        add_real = q_real * real + q_imag * imag
        add_imag = q_imag * real - q_real * imag
        first_real = add_real if first_real is None else first_real + add_real
        first_imag = add_imag if first_imag is None else first_imag + add_imag
    swapped = later == 0
    grad_out[0, 0] = jnp.where(swapped, last_real, first_real)
    grad_out[0, 1] = jnp.where(swapped, last_imag, first_imag)
    grad_out[1, 0] = jnp.where(swapped, first_real, last_real)
    grad_out[1, 1] = jnp.where(swapped, first_imag, last_imag)
    halo_v.up.wait_recv()
    p += col_term(rim.at[4], right_matrix(bank, band[1, 1, 0]))
    halo_v.down.wait_recv()
    p += col_term(rim.at[5], right_matrix(bank, band[1, 1, 2]))
    for angle in range(2):
        for part in range(2):
            exit_out[angle, part] = from_angle(p, angle, part).astype(jnp.bfloat16)
    for halo in (halo_u, halo_g, halo_v, halo_h):
        halo.wait_send()


def call(body, outs, arrays, width, number):
    field = (2, 2, width, width)
    smem = pl.BlockSpec(memory_space=pltpu.SMEM)
    vmem = pl.BlockSpec(memory_space=pltpu.VMEM)
    return pl.pallas_call(
        body,
        out_shape=outs,
        in_specs=[smem] * 3 + [vmem] * (len(arrays) - 3),
        out_specs=[vmem] * len(outs),
        scratch_shapes=[
            pltpu.VMEM(field, jnp.bfloat16),
            pltpu.VMEM(field, jnp.bfloat16),
            pltpu.VMEM(field, jnp.bfloat16),
            pltpu.VMEM((8, *field), jnp.bfloat16),
            pltpu.SemaphoreType.DMA((8,)),
            pltpu.SemaphoreType.DMA((8,)),
        ]
        + [pltpu.VMEM(field, jnp.bfloat16)] * number,
        compiler_params=pltpu.CompilerParams(
            collective_id=number, has_side_effects=True, vmem_limit_bytes=VMEM_LIMIT
        ),
    )(*arrays)


def swap(row_step, col_step, rows, cols, u, q, u_out, q_out, send, recv):
    row, col = lax.axis_index("row"), lax.axis_index("col")
    ahead = (lax.rem(row + row_step, rows), lax.rem(col + col_step, cols))
    behind = (lax.rem(row + rows - row_step, rows), lax.rem(col + cols - col_step, cols))
    barrier = pltpu.get_barrier_semaphore()
    for other in (ahead, behind):
        pl.semaphore_signal(barrier, inc=1, device_id=other, device_id_type=MESH)
    met(2)
    copies = [
        pltpu.make_async_remote_copy(
            src_ref=source,
            dst_ref=target,
            send_sem=send.at[slot],
            recv_sem=recv.at[slot],
            device_id=other,
            device_id_type=MESH,
        )
        for slot, (source, target, other) in enumerate(((u, u_out, ahead), (q, q_out, behind)))
    ]
    for copy in copies:
        copy.start()
    for copy in copies:
        copy.wait()


def move(row_step, col_step, rows, cols, u, q):
    if row_step == 0 and col_step == 0:
        return u, q
    vmem = pl.BlockSpec(memory_space=pltpu.VMEM)
    return pl.pallas_call(
        functools.partial(swap, row_step, col_step, rows, cols),
        out_shape=[jax.ShapeDtypeStruct(u.shape, u.dtype)] * 2,
        in_specs=[vmem] * 2,
        out_specs=[vmem] * 2,
        scratch_shapes=[pltpu.SemaphoreType.DMA((2,)), pltpu.SemaphoreType.DMA((2,))],
        compiler_params=pltpu.CompilerParams(
            collective_id=1 + row_step * SHIFTS + col_step,
            has_side_effects=True,
            vmem_limit_bytes=VMEM_LIMIT,
        ),
    )(u, q)


def local(rows, cols, obj, bank, band_index, tilt, tile_shift, slice_order, cot):
    width = bank.shape[2]
    field = jax.ShapeDtypeStruct(cot.shape, jnp.bfloat16)
    part = jax.ShapeDtypeStruct(cot.shape[1:], jnp.bfloat16)
    u_0, u_1, q_0, q_1, psi = call(
        functools.partial(first, rows, cols),
        (part, part, part, part, field),
        (slice_order, band_index, tilt, obj, bank, cot),
        width,
        0,
    )
    choice = tile_shift[:, 0] * SHIFTS + tile_shift[:, 1]
    branches = [
        functools.partial(move, row_step, col_step, rows, cols)
        for row_step in range(SHIFTS)
        for col_step in range(SHIFTS)
    ]
    u_0, q_0 = lax.switch(choice[0], branches, u_0, q_0)
    u_1, q_1 = lax.switch(choice[1], branches, u_1, q_1)
    exit_field, grad = call(
        functools.partial(second, rows, cols),
        (field, jax.ShapeDtypeStruct(obj.shape, jnp.float32)),
        (slice_order, band_index, tilt, obj, bank, u_0, u_1, q_0, q_1, psi),
        width,
        1,
    )
    return exit_field, grad


def solution(mesh):
    field = P(None, None, "row", "col")
    return jax.shard_map(
        functools.partial(local, mesh.shape["row"], mesh.shape["col"]),
        mesh=mesh,
        in_specs=(field, P(), P(), P(), P(), P(), field),
        out_specs=(field, field),
        check_vma=False,
    )
```

```python
import functools
import math

import jax
import jax.numpy as jnp
from jax import lax
from jax.experimental import pallas as pl
from jax.experimental.pallas import tpu as pltpu
from jax.sharding import PartitionSpec as P

MESH = pl.DeviceIdType.MESH
SHIFTS = 8
GROUP = 8
VMEM_LIMIT = 16 << 20


def left_matrix(bank, index):
    real, imag = bank[index, 0], bank[index, 1]
    return jnp.concatenate(
        [jnp.concatenate([real, -imag], axis=1), jnp.concatenate([imag, real], axis=1)], axis=0
    )


def left_adjoint(bank, index):
    real = bank[index, 0].astype(jnp.float32).T.astype(jnp.bfloat16)
    imag = bank[index, 1].astype(jnp.float32).T.astype(jnp.bfloat16)
    return jnp.concatenate(
        [jnp.concatenate([real, imag], axis=1), jnp.concatenate([-imag, real], axis=1)], axis=0
    )


def right_matrix(bank, index):
    real, imag = bank[index, 0], bank[index, 1]
    return jnp.concatenate(
        [jnp.concatenate([real, imag], axis=1), jnp.concatenate([-imag, real], axis=1)], axis=0
    )


def by_component(field):
    return jnp.concatenate(
        [
            jnp.concatenate([field[0][0], field[1][0]], axis=1),
            jnp.concatenate([field[0][1], field[1][1]], axis=1),
        ],
        axis=0,
    )


def by_angle(field):
    return jnp.concatenate(
        [
            jnp.concatenate([field[0][0], field[0][1]], axis=1),
            jnp.concatenate([field[1][0], field[1][1]], axis=1),
        ],
        axis=0,
    )


def row_term(matrix, field):
    return jnp.dot(matrix, by_component(field), preferred_element_type=jnp.float32)


def col_term(field, matrix):
    return jnp.dot(by_angle(field), matrix, preferred_element_type=jnp.float32)


def col_adjoint_term(field, matrix):
    return lax.dot_general(
        by_angle(field), matrix, (((1,), (1,)), ((), ())), preferred_element_type=jnp.float32
    )


def from_component(total, angle, part):
    n = total.shape[0] // 2
    return total[part * n : (part + 1) * n, angle * n : (angle + 1) * n]


def from_angle(total, angle, part):
    n = total.shape[0] // 2
    return total[angle * n : (angle + 1) * n, part * n : (part + 1) * n]


def incident(tilt, row_start, col_start, period, width):
    line = lax.broadcasted_iota(jnp.int32, (8, width), 0)
    spot = lax.broadcasted_iota(jnp.int32, (8, width), 1)
    rate = jnp.where(
        line == 0,
        tilt[0, 0],
        jnp.where(line == 1, tilt[0, 1], jnp.where(line == 2, tilt[1, 0], tilt[1, 1])),
    )
    start = jnp.where(line % 2 == 0, row_start, col_start)
    turns = (rate * (start + spot)) & (period - 1)
    phase = turns.astype(jnp.float32) * (2.0 * math.pi / period)
    cos, sin = jnp.cos(phase), jnp.sin(phase)
    cos_t, sin_t = cos.T, sin.T
    fields = []
    for angle in range(2):
        row_cos = cos_t[:, 2 * angle : 2 * angle + 1]
        row_sin = sin_t[:, 2 * angle : 2 * angle + 1]
        col_cos = cos[2 * angle + 1 : 2 * angle + 2, :]
        col_sin = sin[2 * angle + 1 : 2 * angle + 2, :]
        fields.append(
            (
                (row_cos * col_cos - row_sin * col_sin).astype(jnp.bfloat16),
                (row_sin * col_cos + row_cos * col_sin).astype(jnp.bfloat16),
            )
        )
    return fields


def pair(ref):
    return ref.at[0], ref.at[1]


class Place:
    def __init__(self, rows, cols):
        self.rows, self.cols = rows, cols
        self.group = min(GROUP, cols // 2)
        self.row, self.col = lax.axis_index("row"), lax.axis_index("col")
        self.spot = lax.rem(self.col, self.group)
        self.base = self.col - self.spot
        self.at_start = self.spot == 0
        self.at_end = self.spot == self.group - 1

    def beside(self, axis, step):
        if axis == "row":
            return lax.rem(self.row + self.rows + step, self.rows), self.col
        return self.row, lax.rem(self.col + self.cols + step, self.cols)

    def in_group(self, step):
        return self.row, lax.rem(self.base + self.cols + step, self.cols)

    def greet(self):
        barrier = pltpu.get_barrier_semaphore()

        def hail(device):
            pl.semaphore_signal(barrier, inc=1, device_id=device, device_id_type=MESH)

        for axis, step in (("row", 1), ("row", -1), ("row", 2), ("row", -2), ("col", 1), ("col", -1)):
            hail(self.beside(axis, step))

        @pl.when(self.at_start)
        def _():
            hail(self.in_group(self.group - 1))

        @pl.when(self.at_end)
        def _():
            hail(self.in_group(0))

    def met(self):
        edge = (self.at_start | self.at_end).astype(jnp.int32)
        pl.semaphore_wait(pltpu.get_barrier_semaphore(), 6 + edge)


class Rows:
    def __init__(self, place, source, rims, steps, slot, send, recv):
        self.copies = []
        self.got = [pair(rim) for rim in rims]
        for target, step in zip(self.got, steps):
            for angle in range(2):
                here = slot + len(self.copies)
                self.copies.append(
                    pltpu.make_async_remote_copy(
                        src_ref=source[angle],
                        dst_ref=target[angle],
                        send_sem=send.at[here],
                        recv_sem=recv.at[here],
                        device_id=place.beside("row", step),
                        device_id_type=MESH,
                    )
                )

    def start(self):
        for copy in self.copies:
            copy.start()

    def wait(self, side):
        self.copies[2 * side].wait_recv()
        self.copies[2 * side + 1].wait_recv()

    def wait_send(self):
        for copy in self.copies:
            copy.wait_send()


def choose(odd, moved, still):
    return [
        [jnp.where(odd[angle], moved[angle][part], still[angle][part]) for part in range(2)]
        for angle in range(2)
    ]


class Cols:
    def __init__(self, place, source, rim, slot, send, recv, stop, stop_send, stop_recv, number):
        self.place = place
        self.low, self.high = pair(rim.at[0]), pair(rim.at[1])
        stop = stop.at[number]

        def copy(src, dst, send_sem, recv_sem, device):
            return pltpu.make_async_remote_copy(
                src_ref=src,
                dst_ref=dst,
                send_sem=send_sem,
                recv_sem=recv_sem,
                device_id=device,
                device_id_type=MESH,
            )

        last = place.group - 1
        self.direct, self.split, self.onward = [], [], []
        for side, (target, step, edge, other, onward) in enumerate(
            (
                (self.low, 1, place.at_end, place.in_group(0), place.in_group(place.group)),
                (self.high, -1, place.at_start, place.in_group(last), place.in_group(-1)),
            )
        ):
            near = place.beside("col", step)
            here = slot + 2 * side
            self.direct.append(copy(source[0], target[0], send.at[here], recv.at[here], near))
            here += 1
            plain = copy(source[1], target[1], send.at[here], recv.at[here], near)
            turned = copy(source[1], stop, send.at[here], stop_recv.at[number], other)
            self.split.append((edge, plain, turned))
            relay = place.at_start if side == 0 else place.at_end
            self.onward.append(
                (relay, turned, copy(stop, target[1], stop_send.at[number], recv.at[here], onward))
            )

    def start_split(self):
        for edge, plain, turned in self.split:

            @pl.when(edge)
            def _():
                turned.start()

            @pl.when(jnp.logical_not(edge))
            def _():
                plain.start()

    def start_direct(self):
        for copy in self.direct:
            copy.start()

    def relay(self):
        for edge, turned, onward in self.onward:

            @pl.when(edge)
            def _():
                turned.wait_recv()
                onward.start()

    def wait_low(self):
        self.direct[0].wait_recv()
        self.split[0][1].wait_recv()

    def wait_high(self):
        self.direct[1].wait_recv()
        self.split[1][1].wait_recv()

    def wait_send(self):
        for copy in self.direct:
            copy.wait_send()
        for _, plain, _ in self.split:
            plain.wait_send()
        for edge, _, onward in self.onward:

            @pl.when(edge)
            def _():
                onward.wait_send()


def put(field, total, pick):
    for angle in range(2):
        for part in range(2):
            field[angle][part] = pick(total, angle, part).astype(jnp.bfloat16)


def first(rows, cols, *refs):
    order, band, tilt, shift, obj_hbm, bank_hbm, cot_hbm = refs[:7]
    u_0, u_1, q_0, q_1, psi_out = refs[7:12]
    mine, rim, stop, send, recv, stop_send, stop_recv, obj, bank, cot, load = refs[12:]
    odd = [shift[angle, 0] % 2 == 1 for angle in range(2)]
    u_out, q_out = (u_0, u_1), (q_0, q_1)
    place = Place(rows, cols)
    place.greet()
    loads = [
        pltpu.make_async_copy(source, target, load.at[number])
        for number, (source, target) in enumerate(
            ((obj_hbm, obj), (cot_hbm, cot), (bank_hbm, bank))
        )
    ]
    for copy in loads:
        copy.start()
    width = bank.shape[2]
    here, later = order[0], order[1]
    fields = incident(tilt, place.row * width, place.col * width, rows * width, width)
    u_mine, v_mine, h_mine = pair(mine.at[0]), pair(mine.at[1]), pair(mine.at[2])
    g_mine = pair(cot)
    loads[0].wait()
    t_real, t_imag = obj[here, 0], obj[here, 1]
    for angle in range(2):
        real = fields[angle][0].astype(jnp.float32)
        imag = fields[angle][1].astype(jnp.float32)
        u_mine[angle][0] = (t_real * real - t_imag * imag).astype(jnp.bfloat16)
        u_mine[angle][1] = (t_real * imag + t_imag * real).astype(jnp.bfloat16)
    loads[1].wait()
    place.met()
    relays = (stop, stop_send, stop_recv)
    halo_u = Rows(place, u_mine, (rim.at[0], rim.at[1]), (1, -1), 0, send, recv)
    halo_g = Cols(place, g_mine, rim.at[pl.ds(2, 2)], 4, send, recv, *relays, 0)
    halo_v = Cols(place, v_mine, rim.at[pl.ds(4, 2)], 8, send, recv, *relays, 1)
    halo_h = Rows(place, h_mine, (rim.at[6], rim.at[7], rim.at[8]), (1, -1, -2), 12, send, recv)
    halo_g.start_split()
    halo_u.start()
    halo_g.start_direct()
    loads[2].wait()
    v = row_term(left_matrix(bank, band[0, 0, 1]), u_mine)
    h = col_adjoint_term(g_mine, right_matrix(bank, band[1, 1, 1]))
    halo_g.relay()
    halo_u.wait(0)
    v += row_term(left_matrix(bank, band[0, 0, 0]), halo_u.got[0])
    halo_u.wait(1)
    v += row_term(left_matrix(bank, band[0, 0, 2]), halo_u.got[1])
    put(v_mine, v, from_component)
    halo_v.start_split()
    halo_v.start_direct()
    p = col_term(v_mine, right_matrix(bank, band[0, 1, 1]))
    halo_v.relay()
    halo_g.wait_low()
    h += col_adjoint_term(halo_g.low, right_matrix(bank, band[1, 1, 2]))
    halo_g.wait_high()
    h += col_adjoint_term(halo_g.high, right_matrix(bank, band[1, 1, 0]))
    put(h_mine, h, from_angle)
    halo_h.start()
    halo_h.wait(1)
    middle = choose(odd, halo_h.got[1], h_mine)
    q = row_term(left_adjoint(bank, band[1, 0, 1]), middle)
    halo_h.wait(0)
    q += row_term(left_adjoint(bank, band[1, 0, 2]), choose(odd, h_mine, halo_h.got[0]))
    halo_h.wait(2)
    q += row_term(left_adjoint(bank, band[1, 0, 0]), choose(odd, halo_h.got[2], halo_h.got[1]))
    put(q_out, q, from_component)
    halo_v.wait_low()
    p += col_term(halo_v.low, right_matrix(bank, band[0, 1, 0]))
    halo_v.wait_high()
    p += col_term(halo_v.high, right_matrix(bank, band[0, 1, 2]))
    s_real, s_imag = obj[later, 0], obj[later, 1]
    for angle in range(2):
        real = from_angle(p, angle, 0).astype(jnp.bfloat16)
        imag = from_angle(p, angle, 1).astype(jnp.bfloat16)
        psi_out[angle, 0] = real
        psi_out[angle, 1] = imag
        real, imag = real.astype(jnp.float32), imag.astype(jnp.float32)
        u_out[angle][0] = (s_real * real - s_imag * imag).astype(jnp.bfloat16)
        u_out[angle][1] = (s_real * imag + s_imag * real).astype(jnp.bfloat16)
    for halo in (halo_u, halo_g, halo_v, halo_h):
        halo.wait_send()


def second(rows, cols, *refs):
    order, band, tilt, shift, obj, bank, u_0, u_1, q_0, q_1, psi, exit_out, grad_out = refs[:13]
    mine, rim, stop, send, recv, stop_send, stop_recv = refs[13:]
    odd = [shift[angle, 0] % 2 == 1 for angle in range(2)]
    u, q = (u_0, u_1), (q_0, q_1)
    place = Place(rows, cols)
    place.greet()
    width = bank.shape[2]
    later = order[1]
    g_mine, v_mine, h_mine = pair(mine.at[0]), pair(mine.at[1]), pair(mine.at[2])
    s_real, s_imag = obj[later, 0], obj[later, 1]
    last_real = None
    last_imag = None
    for angle in range(2):
        q_real, q_imag = q[angle][0].astype(jnp.float32), q[angle][1].astype(jnp.float32)
        g_mine[angle][0] = (q_real * s_real + q_imag * s_imag).astype(jnp.bfloat16)
        g_mine[angle][1] = (q_imag * s_real - q_real * s_imag).astype(jnp.bfloat16)
        real, imag = psi[angle, 0].astype(jnp.float32), psi[angle, 1].astype(jnp.float32)
        add_real = q_real * real + q_imag * imag
        add_imag = q_imag * real - q_real * imag
        last_real = add_real if last_real is None else last_real + add_real
        last_imag = add_imag if last_imag is None else last_imag + add_imag
    place.met()
    relays = (stop, stop_send, stop_recv)
    halo_u = Rows(place, u, (rim.at[0], rim.at[1], rim.at[8]), (1, -1, 2), 12, send, recv)
    halo_g = Cols(place, g_mine, rim.at[pl.ds(2, 2)], 4, send, recv, *relays, 0)
    halo_v = Cols(place, v_mine, rim.at[pl.ds(4, 2)], 8, send, recv, *relays, 1)
    halo_h = Rows(place, h_mine, (rim.at[6], rim.at[7]), (1, -1), 0, send, recv)
    halo_g.start_split()
    halo_u.start()
    halo_g.start_direct()
    h = col_adjoint_term(g_mine, right_matrix(bank, band[0, 1, 1]))
    halo_g.relay()
    halo_u.wait(0)
    v = row_term(left_matrix(bank, band[1, 0, 1]), choose(odd, halo_u.got[0], u))
    halo_u.wait(1)
    v += row_term(left_matrix(bank, band[1, 0, 2]), choose(odd, u, halo_u.got[1]))
    halo_u.wait(2)
    v += row_term(left_matrix(bank, band[1, 0, 0]), choose(odd, halo_u.got[2], halo_u.got[0]))
    put(v_mine, v, from_component)
    halo_v.start_split()
    halo_v.start_direct()
    p = col_term(v_mine, right_matrix(bank, band[1, 1, 1]))
    halo_v.relay()
    halo_g.wait_low()
    h += col_adjoint_term(halo_g.low, right_matrix(bank, band[0, 1, 2]))
    halo_g.wait_high()
    h += col_adjoint_term(halo_g.high, right_matrix(bank, band[0, 1, 0]))
    put(h_mine, h, from_angle)
    halo_h.start()
    fields = incident(tilt, place.row * width, place.col * width, rows * width, width)
    b = row_term(left_adjoint(bank, band[0, 0, 1]), h_mine)
    halo_h.wait(0)
    b += row_term(left_adjoint(bank, band[0, 0, 2]), halo_h.got[0])
    halo_h.wait(1)
    b += row_term(left_adjoint(bank, band[0, 0, 0]), halo_h.got[1])
    first_real = None
    first_imag = None
    for angle in range(2):
        q_real = from_component(b, angle, 0).astype(jnp.bfloat16).astype(jnp.float32)
        q_imag = from_component(b, angle, 1).astype(jnp.bfloat16).astype(jnp.float32)
        real, imag = fields[angle][0].astype(jnp.float32), fields[angle][1].astype(jnp.float32)
        add_real = q_real * real + q_imag * imag
        add_imag = q_imag * real - q_real * imag
        first_real = add_real if first_real is None else first_real + add_real
        first_imag = add_imag if first_imag is None else first_imag + add_imag
    swapped = later == 0
    grad_out[0, 0] = jnp.where(swapped, last_real, first_real)
    grad_out[0, 1] = jnp.where(swapped, last_imag, first_imag)
    grad_out[1, 0] = jnp.where(swapped, first_real, last_real)
    grad_out[1, 1] = jnp.where(swapped, first_imag, last_imag)
    halo_v.wait_low()
    p += col_term(halo_v.low, right_matrix(bank, band[1, 1, 0]))
    halo_v.wait_high()
    p += col_term(halo_v.high, right_matrix(bank, band[1, 1, 2]))
    put(pair(exit_out), p, from_angle)
    for halo in (halo_u, halo_g, halo_v, halo_h):
        halo.wait_send()


def call(body, outs, arrays, held, number):
    width = held[0].shape[2]
    field = (2, 2, width, width)
    smem = pl.BlockSpec(memory_space=pltpu.SMEM)
    vmem = pl.BlockSpec(memory_space=pltpu.VMEM)
    specs = [smem] * 4 + [vmem] * (len(arrays) - 4)
    extra = []
    if len(held) == 3:
        specs = [smem] * 4 + [pl.BlockSpec(memory_space=pltpu.HBM)] * 3
        extra = [pltpu.VMEM(array.shape, array.dtype) for array in arrays[4:]]
        extra.append(pltpu.SemaphoreType.DMA((3,)))
    return pl.pallas_call(
        body,
        out_shape=outs,
        in_specs=specs,
        out_specs=[vmem] * len(outs),
        scratch_shapes=[
            pltpu.VMEM((3, *field), jnp.bfloat16),
            pltpu.VMEM((9, *field), jnp.bfloat16),
            pltpu.VMEM((2, *field[1:]), jnp.bfloat16),
            pltpu.SemaphoreType.DMA((18,)),
            pltpu.SemaphoreType.DMA((18,)),
            pltpu.SemaphoreType.DMA((2,)),
            pltpu.SemaphoreType.DMA((2,)),
            *extra,
        ],
        compiler_params=pltpu.CompilerParams(
            collective_id=number, has_side_effects=True, vmem_limit_bytes=VMEM_LIMIT
        ),
    )(*arrays)


def swap(row_step, col_step, rows, cols, u, q, u_out, q_out, send, recv):
    row, col = lax.axis_index("row"), lax.axis_index("col")
    ahead = (lax.rem(row + row_step, rows), lax.rem(col + col_step, cols))
    behind = (lax.rem(row + -row_step % rows, rows), lax.rem(col + -col_step % cols, cols))
    barrier = pltpu.get_barrier_semaphore()
    for other in (ahead, behind):
        pl.semaphore_signal(barrier, inc=1, device_id=other, device_id_type=MESH)
    pl.semaphore_wait(barrier, 2)
    copies = [
        pltpu.make_async_remote_copy(
            src_ref=source,
            dst_ref=target,
            send_sem=send.at[slot],
            recv_sem=recv.at[slot],
            device_id=other,
            device_id_type=MESH,
        )
        for slot, (source, target, other) in enumerate(((u, u_out, ahead), (q, q_out, behind)))
    ]
    for copy in copies:
        copy.start()
    for copy in copies:
        copy.wait()


def move(row_step, col_step, rows, cols, u, q):
    if row_step == 0 and col_step == 0:
        return u, q
    vmem = pl.BlockSpec(memory_space=pltpu.VMEM)
    return pl.pallas_call(
        functools.partial(swap, row_step, col_step, rows, cols),
        out_shape=[jax.ShapeDtypeStruct(u.shape, u.dtype)] * 2,
        in_specs=[vmem] * 2,
        out_specs=[vmem] * 2,
        scratch_shapes=[pltpu.SemaphoreType.DMA((2,)), pltpu.SemaphoreType.DMA((2,))],
        compiler_params=pltpu.CompilerParams(
            collective_id=1 + row_step // 2 * SHIFTS + col_step,
            has_side_effects=True,
            vmem_limit_bytes=VMEM_LIMIT,
        ),
    )(u, q)


def local(rows, cols, obj, bank, band_index, tilt, tile_shift, slice_order, cot):
    field = jax.ShapeDtypeStruct(cot.shape, jnp.bfloat16)
    part = jax.ShapeDtypeStruct(cot.shape[1:], jnp.bfloat16)
    u_0, u_1, q_0, q_1, psi = call(
        functools.partial(first, rows, cols),
        (part, part, part, part, field),
        (slice_order, band_index, tilt, tile_shift, obj, bank, cot),
        (bank, obj, cot),
        0,
    )
    choice = tile_shift[:, 0] // 2 * SHIFTS + tile_shift[:, 1]
    branches = [
        functools.partial(move, row_step, col_step, rows, cols)
        for row_step in range(0, SHIFTS, 2)
        for col_step in range(SHIFTS)
    ]
    u_0, q_0 = lax.switch(choice[0], branches, u_0, q_0)
    u_1, q_1 = lax.switch(choice[1], branches, u_1, q_1)
    exit_field, grad = call(
        functools.partial(second, rows, cols),
        (field, jax.ShapeDtypeStruct(obj.shape, jnp.float32)),
        (slice_order, band_index, tilt, tile_shift, obj, bank, u_0, u_1, q_0, q_1, psi),
        (bank,),
        1,
    )
    return exit_field, grad


def solution(mesh):
    field = P(None, None, "row", "col")
    return jax.shard_map(
        functools.partial(local, mesh.shape["row"], mesh.shape["col"]),
        mesh=mesh,
        in_specs=(field, P(), P(), P(), P(), P(), field),
        out_specs=(field, field),
        check_vma=False,
    )
```

```python
import functools
import math

import jax
import jax.numpy as jnp
from jax import lax
from jax.experimental import pallas as pl
from jax.experimental.pallas import tpu as pltpu
from jax.sharding import PartitionSpec as P

MESH = pl.DeviceIdType.MESH
SHIFTS = 8
GROUP = 8
VMEM_LIMIT = 16 << 20
FIRST_LIMIT = 61 << 20


def left_matrix(bank, index):
    real, imag = bank[index, 0], bank[index, 1]
    return jnp.concatenate(
        [jnp.concatenate([real, -imag], axis=1), jnp.concatenate([imag, real], axis=1)], axis=0
    )


def left_adjoint(bank, index):
    real = bank[index, 0].astype(jnp.float32).T.astype(jnp.bfloat16)
    imag = bank[index, 1].astype(jnp.float32).T.astype(jnp.bfloat16)
    return jnp.concatenate(
        [jnp.concatenate([real, imag], axis=1), jnp.concatenate([-imag, real], axis=1)], axis=0
    )


def right_matrix(bank, index):
    real, imag = bank[index, 0], bank[index, 1]
    return jnp.concatenate(
        [jnp.concatenate([real, imag], axis=1), jnp.concatenate([-imag, real], axis=1)], axis=0
    )


def by_component(field):
    return jnp.concatenate(
        [
            jnp.concatenate([field[0][0], field[1][0]], axis=1),
            jnp.concatenate([field[0][1], field[1][1]], axis=1),
        ],
        axis=0,
    )


def by_angle(field):
    return jnp.concatenate(
        [
            jnp.concatenate([field[0][0], field[0][1]], axis=1),
            jnp.concatenate([field[1][0], field[1][1]], axis=1),
        ],
        axis=0,
    )


def row_term(matrix, field):
    return jnp.dot(matrix, by_component(field), preferred_element_type=jnp.float32)


def col_term(field, matrix):
    return jnp.dot(by_angle(field), matrix, preferred_element_type=jnp.float32)


def col_adjoint_term(field, matrix):
    return lax.dot_general(
        by_angle(field), matrix, (((1,), (1,)), ((), ())), preferred_element_type=jnp.float32
    )


def from_component(total, angle, part):
    n = total.shape[0] // 2
    return total[part * n : (part + 1) * n, angle * n : (angle + 1) * n]


def from_angle(total, angle, part):
    n = total.shape[0] // 2
    return total[angle * n : (angle + 1) * n, part * n : (part + 1) * n]


def incident(tilt, row_start, col_start, period, width):
    line = lax.broadcasted_iota(jnp.int32, (8, width), 0)
    spot = lax.broadcasted_iota(jnp.int32, (8, width), 1)
    rate = jnp.where(
        line == 0,
        tilt[0, 0],
        jnp.where(line == 1, tilt[0, 1], jnp.where(line == 2, tilt[1, 0], tilt[1, 1])),
    )
    start = jnp.where(line % 2 == 0, row_start, col_start)
    turns = (rate * (start + spot)) & (period - 1)
    phase = turns.astype(jnp.float32) * (2.0 * math.pi / period)
    cos, sin = jnp.cos(phase), jnp.sin(phase)
    cos_t, sin_t = cos.T, sin.T
    fields = []
    for angle in range(2):
        row_cos = cos_t[:, 2 * angle : 2 * angle + 1]
        row_sin = sin_t[:, 2 * angle : 2 * angle + 1]
        col_cos = cos[2 * angle + 1 : 2 * angle + 2, :]
        col_sin = sin[2 * angle + 1 : 2 * angle + 2, :]
        fields.append(
            (
                (row_cos * col_cos - row_sin * col_sin).astype(jnp.bfloat16),
                (row_sin * col_cos + row_cos * col_sin).astype(jnp.bfloat16),
            )
        )
    return fields


def pair(ref):
    return ref.at[0], ref.at[1]


class Place:
    def __init__(self, rows, cols):
        self.rows, self.cols = rows, cols
        self.group = min(GROUP, cols // 2)
        self.row, self.col = lax.axis_index("row"), lax.axis_index("col")
        self.spot = lax.rem(self.col, self.group)
        self.base = self.col - self.spot
        self.at_start = self.spot == 0
        self.at_end = self.spot == self.group - 1

    def beside(self, axis, step):
        if axis == "row":
            return lax.rem(self.row + self.rows + step, self.rows), self.col
        return self.row, lax.rem(self.col + self.cols + step, self.cols)

    def in_group(self, step):
        return self.row, lax.rem(self.base + self.cols + step, self.cols)

    def greet(self):
        barrier = pltpu.get_barrier_semaphore()

        def hail(device):
            pl.semaphore_signal(barrier, inc=1, device_id=device, device_id_type=MESH)

        for axis, step in (("row", 1), ("row", -1), ("row", 2), ("row", -2), ("col", 1), ("col", -1)):
            hail(self.beside(axis, step))

        @pl.when(self.at_start)
        def _():
            hail(self.in_group(self.group - 1))

        @pl.when(self.at_end)
        def _():
            hail(self.in_group(0))

    def met(self):
        edge = (self.at_start | self.at_end).astype(jnp.int32)
        pl.semaphore_wait(pltpu.get_barrier_semaphore(), 6 + edge)


class Rows:
    def __init__(self, place, source, rims, steps, slot, send, recv):
        self.copies = []
        self.got = [pair(rim) for rim in rims]
        for target, step in zip(self.got, steps):
            for angle in range(2):
                here = slot + len(self.copies)
                self.copies.append(
                    pltpu.make_async_remote_copy(
                        src_ref=source[angle],
                        dst_ref=target[angle],
                        send_sem=send.at[here],
                        recv_sem=recv.at[here],
                        device_id=place.beside("row", step),
                        device_id_type=MESH,
                    )
                )

    def start(self):
        for copy in self.copies:
            copy.start()

    def wait(self, side):
        self.copies[2 * side].wait_recv()
        self.copies[2 * side + 1].wait_recv()

    def wait_send(self):
        for copy in self.copies:
            copy.wait_send()


def choose(odd, moved, still):
    return [
        [jnp.where(odd[angle], moved[angle][part], still[angle][part]) for part in range(2)]
        for angle in range(2)
    ]


class Cols:
    def __init__(self, place, source, rim, slot, send, recv, stop, stop_send, stop_recv, number):
        self.place = place
        self.low, self.high = pair(rim.at[0]), pair(rim.at[1])
        stop = stop.at[number]

        def copy(src, dst, send_sem, recv_sem, device):
            return pltpu.make_async_remote_copy(
                src_ref=src,
                dst_ref=dst,
                send_sem=send_sem,
                recv_sem=recv_sem,
                device_id=device,
                device_id_type=MESH,
            )

        last = place.group - 1
        self.direct, self.split, self.onward = [], [], []
        for side, (target, step, edge, other, onward) in enumerate(
            (
                (self.low, 1, place.at_end, place.in_group(0), place.in_group(place.group)),
                (self.high, -1, place.at_start, place.in_group(last), place.in_group(-1)),
            )
        ):
            near = place.beside("col", step)
            here = slot + 2 * side
            self.direct.append(copy(source[0], target[0], send.at[here], recv.at[here], near))
            here += 1
            plain = copy(source[1], target[1], send.at[here], recv.at[here], near)
            turned = copy(source[1], stop, send.at[here], stop_recv.at[number], other)
            self.split.append((edge, plain, turned))
            relay = place.at_start if side == 0 else place.at_end
            self.onward.append(
                (relay, turned, copy(stop, target[1], stop_send.at[number], recv.at[here], onward))
            )

    def start_split(self):
        for edge, plain, turned in self.split:

            @pl.when(edge)
            def _():
                turned.start()

            @pl.when(jnp.logical_not(edge))
            def _():
                plain.start()

    def start_direct(self):
        for copy in self.direct:
            copy.start()

    def relay(self):
        for edge, turned, onward in self.onward:

            @pl.when(edge)
            def _():
                turned.wait_recv()
                onward.start()

    def wait_low(self):
        self.direct[0].wait_recv()
        self.split[0][1].wait_recv()

    def wait_high(self):
        self.direct[1].wait_recv()
        self.split[1][1].wait_recv()

    def wait_send(self):
        for copy in self.direct:
            copy.wait_send()
        for _, plain, _ in self.split:
            plain.wait_send()
        for edge, _, onward in self.onward:

            @pl.when(edge)
            def _():
                onward.wait_send()


def put(field, total, pick):
    for angle in range(2):
        for part in range(2):
            field[angle][part] = pick(total, angle, part).astype(jnp.bfloat16)


def first(rows, cols, *refs):
    order, band, tilt, shift, obj_hbm, bank_hbm, cot_hbm = refs[:7]
    u_0, u_1, q_0, q_1, psi_out = refs[7:12]
    mine, rim, stop, send, recv, stop_send, stop_recv, obj, bank, cot, load = refs[12:]
    odd = [shift[angle, 0] % 2 == 1 for angle in range(2)]
    u_out, q_out = (u_0, u_1), (q_0, q_1)
    place = Place(rows, cols)
    place.greet()
    loads = [
        pltpu.make_async_copy(source, target, load.at[number])
        for number, (source, target) in enumerate(
            ((obj_hbm, obj), (cot_hbm, cot), (bank_hbm, bank))
        )
    ]
    for copy in loads:
        copy.start()
    width = bank.shape[2]
    here, later = order[0], order[1]
    fields = incident(tilt, place.row * width, place.col * width, rows * width, width)
    u_mine, v_mine, h_mine = pair(mine.at[0]), pair(mine.at[1]), pair(mine.at[2])
    g_mine = pair(cot)
    loads[0].wait()
    t_real, t_imag = obj[here, 0], obj[here, 1]
    for angle in range(2):
        real = fields[angle][0].astype(jnp.float32)
        imag = fields[angle][1].astype(jnp.float32)
        u_mine[angle][0] = (t_real * real - t_imag * imag).astype(jnp.bfloat16)
        u_mine[angle][1] = (t_real * imag + t_imag * real).astype(jnp.bfloat16)
    loads[1].wait()
    place.met()
    relays = (stop, stop_send, stop_recv)
    halo_u = Rows(place, u_mine, (rim.at[0], rim.at[1]), (1, -1), 0, send, recv)
    halo_g = Cols(place, g_mine, rim.at[pl.ds(2, 2)], 4, send, recv, *relays, 0)
    halo_v = Cols(place, v_mine, rim.at[pl.ds(4, 2)], 8, send, recv, *relays, 1)
    halo_h = Rows(place, h_mine, (rim.at[6], rim.at[7], rim.at[8]), (1, -1, -2), 12, send, recv)
    halo_g.start_split()
    halo_u.start()
    halo_g.start_direct()
    loads[2].wait()
    v = row_term(left_matrix(bank, band[0, 0, 1]), u_mine)
    h = col_adjoint_term(g_mine, right_matrix(bank, band[1, 1, 1]))
    halo_g.relay()
    halo_u.wait(0)
    v += row_term(left_matrix(bank, band[0, 0, 0]), halo_u.got[0])
    halo_u.wait(1)
    v += row_term(left_matrix(bank, band[0, 0, 2]), halo_u.got[1])
    put(v_mine, v, from_component)
    halo_v.start_split()
    halo_v.start_direct()
    p = col_term(v_mine, right_matrix(bank, band[0, 1, 1]))
    halo_v.relay()
    halo_g.wait_low()
    h += col_adjoint_term(halo_g.low, right_matrix(bank, band[1, 1, 2]))
    halo_g.wait_high()
    h += col_adjoint_term(halo_g.high, right_matrix(bank, band[1, 1, 0]))
    put(h_mine, h, from_angle)
    halo_h.start()
    halo_h.wait(1)
    middle = choose(odd, halo_h.got[1], h_mine)
    q = row_term(left_adjoint(bank, band[1, 0, 1]), middle)
    halo_h.wait(0)
    q += row_term(left_adjoint(bank, band[1, 0, 2]), choose(odd, h_mine, halo_h.got[0]))
    halo_h.wait(2)
    q += row_term(left_adjoint(bank, band[1, 0, 0]), choose(odd, halo_h.got[2], halo_h.got[1]))
    put(q_out, q, from_component)
    halo_v.wait_low()
    p += col_term(halo_v.low, right_matrix(bank, band[0, 1, 0]))
    halo_v.wait_high()
    p += col_term(halo_v.high, right_matrix(bank, band[0, 1, 2]))
    s_real, s_imag = obj[later, 0], obj[later, 1]
    for angle in range(2):
        real = from_angle(p, angle, 0).astype(jnp.bfloat16)
        imag = from_angle(p, angle, 1).astype(jnp.bfloat16)
        psi_out[angle, 0] = real
        psi_out[angle, 1] = imag
        real, imag = real.astype(jnp.float32), imag.astype(jnp.float32)
        u_out[angle][0] = (s_real * real - s_imag * imag).astype(jnp.bfloat16)
        u_out[angle][1] = (s_real * imag + s_imag * real).astype(jnp.bfloat16)
    for halo in (halo_u, halo_g, halo_v, halo_h):
        halo.wait_send()


def second(rows, cols, *refs):
    order, band, tilt, shift, obj, bank, u_0, u_1, q_0, q_1, psi, exit_out, grad_out = refs[:13]
    mine, rim, stop, send, recv, stop_send, stop_recv = refs[13:]
    odd = [shift[angle, 0] % 2 == 1 for angle in range(2)]
    u, q = (u_0, u_1), (q_0, q_1)
    place = Place(rows, cols)
    place.greet()
    width = bank.shape[2]
    later = order[1]
    g_mine, v_mine, h_mine = pair(mine.at[0]), pair(mine.at[1]), pair(mine.at[2])
    s_real, s_imag = obj[later, 0], obj[later, 1]
    last_real = None
    last_imag = None
    for angle in range(2):
        q_real, q_imag = q[angle][0].astype(jnp.float32), q[angle][1].astype(jnp.float32)
        g_mine[angle][0] = (q_real * s_real + q_imag * s_imag).astype(jnp.bfloat16)
        g_mine[angle][1] = (q_imag * s_real - q_real * s_imag).astype(jnp.bfloat16)
        real, imag = psi[angle, 0].astype(jnp.float32), psi[angle, 1].astype(jnp.float32)
        add_real = q_real * real + q_imag * imag
        add_imag = q_imag * real - q_real * imag
        last_real = add_real if last_real is None else last_real + add_real
        last_imag = add_imag if last_imag is None else last_imag + add_imag
    place.met()
    relays = (stop, stop_send, stop_recv)
    halo_u = Rows(place, u, (rim.at[0], rim.at[1], rim.at[8]), (1, -1, 2), 12, send, recv)
    halo_g = Cols(place, g_mine, rim.at[pl.ds(2, 2)], 4, send, recv, *relays, 0)
    halo_v = Cols(place, v_mine, rim.at[pl.ds(4, 2)], 8, send, recv, *relays, 1)
    halo_h = Rows(place, h_mine, (rim.at[6], rim.at[7]), (1, -1), 0, send, recv)
    halo_g.start_split()
    halo_u.start()
    halo_g.start_direct()
    h = col_adjoint_term(g_mine, right_matrix(bank, band[0, 1, 1]))
    halo_g.relay()
    halo_u.wait(0)
    v = row_term(left_matrix(bank, band[1, 0, 1]), choose(odd, halo_u.got[0], u))
    halo_u.wait(1)
    v += row_term(left_matrix(bank, band[1, 0, 2]), choose(odd, u, halo_u.got[1]))
    halo_u.wait(2)
    v += row_term(left_matrix(bank, band[1, 0, 0]), choose(odd, halo_u.got[2], halo_u.got[0]))
    put(v_mine, v, from_component)
    halo_v.start_split()
    halo_v.start_direct()
    p = col_term(v_mine, right_matrix(bank, band[1, 1, 1]))
    halo_v.relay()
    halo_g.wait_low()
    h += col_adjoint_term(halo_g.low, right_matrix(bank, band[0, 1, 2]))
    halo_g.wait_high()
    h += col_adjoint_term(halo_g.high, right_matrix(bank, band[0, 1, 0]))
    put(h_mine, h, from_angle)
    halo_h.start()
    fields = incident(tilt, place.row * width, place.col * width, rows * width, width)
    b = row_term(left_adjoint(bank, band[0, 0, 1]), h_mine)
    halo_h.wait(0)
    b += row_term(left_adjoint(bank, band[0, 0, 2]), halo_h.got[0])
    halo_h.wait(1)
    b += row_term(left_adjoint(bank, band[0, 0, 0]), halo_h.got[1])
    first_real = None
    first_imag = None
    for angle in range(2):
        q_real = from_component(b, angle, 0).astype(jnp.bfloat16).astype(jnp.float32)
        q_imag = from_component(b, angle, 1).astype(jnp.bfloat16).astype(jnp.float32)
        real, imag = fields[angle][0].astype(jnp.float32), fields[angle][1].astype(jnp.float32)
        add_real = q_real * real + q_imag * imag
        add_imag = q_imag * real - q_real * imag
        first_real = add_real if first_real is None else first_real + add_real
        first_imag = add_imag if first_imag is None else first_imag + add_imag
    swapped = later == 0
    grad_out[0, 0] = jnp.where(swapped, last_real, first_real)
    grad_out[0, 1] = jnp.where(swapped, last_imag, first_imag)
    grad_out[1, 0] = jnp.where(swapped, first_real, last_real)
    grad_out[1, 1] = jnp.where(swapped, first_imag, last_imag)
    halo_v.wait_low()
    p += col_term(halo_v.low, right_matrix(bank, band[1, 1, 0]))
    halo_v.wait_high()
    p += col_term(halo_v.high, right_matrix(bank, band[1, 1, 2]))
    put(pair(exit_out), p, from_angle)
    for halo in (halo_u, halo_g, halo_v, halo_h):
        halo.wait_send()


def call(body, outs, arrays, held, number, limit):
    width = held[0].shape[2]
    field = (2, 2, width, width)
    smem = pl.BlockSpec(memory_space=pltpu.SMEM)
    vmem = pl.BlockSpec(memory_space=pltpu.VMEM)
    specs = [smem] * 4 + [vmem] * (len(arrays) - 4)
    extra = []
    if len(held) == 3:
        specs = [smem] * 4 + [pl.BlockSpec(memory_space=pltpu.HBM)] * 3
        extra = [pltpu.VMEM(array.shape, array.dtype) for array in arrays[4:]]
        extra.append(pltpu.SemaphoreType.DMA((3,)))
    return pl.pallas_call(
        body,
        out_shape=outs,
        in_specs=specs,
        out_specs=[vmem] * len(outs),
        scratch_shapes=[
            pltpu.VMEM((3, *field), jnp.bfloat16),
            pltpu.VMEM((9, *field), jnp.bfloat16),
            pltpu.VMEM((2, *field[1:]), jnp.bfloat16),
            pltpu.SemaphoreType.DMA((18,)),
            pltpu.SemaphoreType.DMA((18,)),
            pltpu.SemaphoreType.DMA((2,)),
            pltpu.SemaphoreType.DMA((2,)),
            *extra,
        ],
        compiler_params=pltpu.CompilerParams(
            collective_id=number, has_side_effects=True, vmem_limit_bytes=limit
        ),
    )(*arrays)


def swap(row_step, col_step, rows, cols, u, q, u_out, q_out, send, recv):
    row, col = lax.axis_index("row"), lax.axis_index("col")
    ahead = (lax.rem(row + row_step, rows), lax.rem(col + col_step, cols))
    behind = (lax.rem(row + -row_step % rows, rows), lax.rem(col + -col_step % cols, cols))
    barrier = pltpu.get_barrier_semaphore()
    for other in (ahead, behind):
        pl.semaphore_signal(barrier, inc=1, device_id=other, device_id_type=MESH)
    pl.semaphore_wait(barrier, 2)
    copies = [
        pltpu.make_async_remote_copy(
            src_ref=source,
            dst_ref=target,
            send_sem=send.at[slot],
            recv_sem=recv.at[slot],
            device_id=other,
            device_id_type=MESH,
        )
        for slot, (source, target, other) in enumerate(((u, u_out, ahead), (q, q_out, behind)))
    ]
    for copy in copies:
        copy.start()
    for copy in copies:
        copy.wait()


def move(row_step, col_step, rows, cols, u, q):
    if row_step == 0 and col_step == 0:
        return u, q
    vmem = pl.BlockSpec(memory_space=pltpu.VMEM)
    return pl.pallas_call(
        functools.partial(swap, row_step, col_step, rows, cols),
        out_shape=[jax.ShapeDtypeStruct(u.shape, u.dtype)] * 2,
        in_specs=[vmem] * 2,
        out_specs=[vmem] * 2,
        scratch_shapes=[pltpu.SemaphoreType.DMA((2,)), pltpu.SemaphoreType.DMA((2,))],
        compiler_params=pltpu.CompilerParams(
            collective_id=1 + row_step // 2 * SHIFTS + col_step,
            has_side_effects=True,
            vmem_limit_bytes=VMEM_LIMIT,
        ),
    )(u, q)


def local(rows, cols, obj, bank, band_index, tilt, tile_shift, slice_order, cot):
    field = jax.ShapeDtypeStruct(cot.shape, jnp.bfloat16)
    part = jax.ShapeDtypeStruct(cot.shape[1:], jnp.bfloat16)
    u_0, u_1, q_0, q_1, psi = call(
        functools.partial(first, rows, cols),
        (part, part, part, part, field),
        (slice_order, band_index, tilt, tile_shift, obj, bank, cot),
        (bank, obj, cot),
        0,
        FIRST_LIMIT,
    )
    choice = [
        (tile_shift[angle, 0] >> 1) * SHIFTS + tile_shift[angle, 1] for angle in range(2)
    ]
    branches = [
        functools.partial(move, row_step, col_step, rows, cols)
        for row_step in range(0, SHIFTS, 2)
        for col_step in range(SHIFTS)
    ]
    u_0, q_0 = lax.switch(choice[0], branches, u_0, q_0)
    u_1, q_1 = lax.switch(choice[1], branches, u_1, q_1)
    exit_field, grad = call(
        functools.partial(second, rows, cols),
        (field, jax.ShapeDtypeStruct(obj.shape, jnp.float32)),
        (slice_order, band_index, tilt, tile_shift, obj, bank, u_0, u_1, q_0, q_1, psi),
        (bank,),
        1,
        VMEM_LIMIT,
    )
    return exit_field, grad


def solution(mesh):
    field = P(None, None, "row", "col")
    return jax.shard_map(
        functools.partial(local, mesh.shape["row"], mesh.shape["col"]),
        mesh=mesh,
        in_specs=(field, P(), P(), P(), P(), P(), field),
        out_specs=(field, field),
        check_vma=False,
    )
```

```python
import functools
import math

import jax
import jax.numpy as jnp
from jax import lax
from jax.extend.core.primitives import cond_p
from jax.experimental import pallas as pl
from jax.experimental.pallas import tpu as pltpu
from jax.sharding import PartitionSpec as P

MESH = pl.DeviceIdType.MESH
SHIFTS = 8
GROUP = 8
VMEM_LIMIT = 16 << 20
FIRST_LIMIT = 61 << 20


def left_matrix(bank, index):
    real, imag = bank[index, 0], bank[index, 1]
    return jnp.concatenate(
        [jnp.concatenate([real, -imag], axis=1), jnp.concatenate([imag, real], axis=1)], axis=0
    )


def left_adjoint(bank, index):
    real = bank[index, 0].astype(jnp.float32).T.astype(jnp.bfloat16)
    imag = bank[index, 1].astype(jnp.float32).T.astype(jnp.bfloat16)
    return jnp.concatenate(
        [jnp.concatenate([real, imag], axis=1), jnp.concatenate([-imag, real], axis=1)], axis=0
    )


def right_matrix(bank, index):
    real, imag = bank[index, 0], bank[index, 1]
    return jnp.concatenate(
        [jnp.concatenate([real, imag], axis=1), jnp.concatenate([-imag, real], axis=1)], axis=0
    )


def by_component(field):
    return jnp.concatenate(
        [
            jnp.concatenate([field[0][0], field[1][0]], axis=1),
            jnp.concatenate([field[0][1], field[1][1]], axis=1),
        ],
        axis=0,
    )


def by_angle(field):
    return jnp.concatenate(
        [
            jnp.concatenate([field[0][0], field[0][1]], axis=1),
            jnp.concatenate([field[1][0], field[1][1]], axis=1),
        ],
        axis=0,
    )


def row_term(matrix, field):
    return jnp.dot(matrix, by_component(field), preferred_element_type=jnp.float32)


def col_term(field, matrix):
    return jnp.dot(by_angle(field), matrix, preferred_element_type=jnp.float32)


def col_adjoint_term(field, matrix):
    return lax.dot_general(
        by_angle(field), matrix, (((1,), (1,)), ((), ())), preferred_element_type=jnp.float32
    )


def from_component(total, angle, part):
    n = total.shape[0] // 2
    return total[part * n : (part + 1) * n, angle * n : (angle + 1) * n]


def from_angle(total, angle, part):
    n = total.shape[0] // 2
    return total[angle * n : (angle + 1) * n, part * n : (part + 1) * n]


def incident(tilt, row_start, col_start, period, width):
    line = lax.broadcasted_iota(jnp.int32, (8, width), 0)
    spot = lax.broadcasted_iota(jnp.int32, (8, width), 1)
    rate = jnp.where(
        line == 0,
        tilt[0, 0],
        jnp.where(line == 1, tilt[0, 1], jnp.where(line == 2, tilt[1, 0], tilt[1, 1])),
    )
    start = jnp.where(line % 2 == 0, row_start, col_start)
    turns = (rate * (start + spot)) & (period - 1)
    phase = turns.astype(jnp.float32) * (2.0 * math.pi / period)
    cos, sin = jnp.cos(phase), jnp.sin(phase)
    cos_t, sin_t = cos.T, sin.T
    fields = []
    for angle in range(2):
        row_cos = cos_t[:, 2 * angle : 2 * angle + 1]
        row_sin = sin_t[:, 2 * angle : 2 * angle + 1]
        col_cos = cos[2 * angle + 1 : 2 * angle + 2, :]
        col_sin = sin[2 * angle + 1 : 2 * angle + 2, :]
        fields.append(
            (
                (row_cos * col_cos - row_sin * col_sin).astype(jnp.bfloat16),
                (row_sin * col_cos + row_cos * col_sin).astype(jnp.bfloat16),
            )
        )
    return fields


def pair(ref):
    return ref.at[0], ref.at[1]


class Place:
    def __init__(self, rows, cols):
        self.rows, self.cols = rows, cols
        self.group = min(GROUP, cols // 2)
        self.row, self.col = lax.axis_index("row"), lax.axis_index("col")
        self.spot = lax.rem(self.col, self.group)
        self.base = self.col - self.spot
        self.at_start = self.spot == 0
        self.at_end = self.spot == self.group - 1

    def beside(self, axis, step):
        if axis == "row":
            return lax.rem(self.row + self.rows + step, self.rows), self.col
        return self.row, lax.rem(self.col + self.cols + step, self.cols)

    def in_group(self, step):
        return self.row, lax.rem(self.base + self.cols + step, self.cols)

    def greet(self):
        barrier = pltpu.get_barrier_semaphore()

        def hail(device):
            pl.semaphore_signal(barrier, inc=1, device_id=device, device_id_type=MESH)

        for axis, step in (("row", 1), ("row", -1), ("row", 2), ("row", -2), ("col", 1), ("col", -1)):
            hail(self.beside(axis, step))

        @pl.when(self.at_start)
        def _():
            hail(self.in_group(self.group - 1))

        @pl.when(self.at_end)
        def _():
            hail(self.in_group(0))

    def met(self):
        edge = (self.at_start | self.at_end).astype(jnp.int32)
        pl.semaphore_wait(pltpu.get_barrier_semaphore(), 6 + edge)


class Rows:
    def __init__(self, place, sources, rims, steps, slot, send, recv):
        self.got = [pair(rim) for rim in rims]
        self.each = len(sources)
        self.copies = []
        for rim, step in zip(rims, steps):
            for part, source in enumerate(sources):
                here = slot + len(self.copies)
                self.copies.append(
                    pltpu.make_async_remote_copy(
                        src_ref=source,
                        dst_ref=rim if self.each == 1 else rim.at[part],
                        send_sem=send.at[here],
                        recv_sem=recv.at[here],
                        device_id=place.beside("row", step),
                        device_id_type=MESH,
                    )
                )

    def start(self):
        for copy in self.copies:
            copy.start()

    def wait(self, side):
        for copy in self.copies[side * self.each : (side + 1) * self.each]:
            copy.wait_recv()

    def wait_send(self):
        for copy in self.copies:
            copy.wait_send()


def choose(odd, moved, still):
    return [
        [jnp.where(odd[angle], moved[angle][part], still[angle][part]) for part in range(2)]
        for angle in range(2)
    ]


class Cols:
    def __init__(self, place, source, rim, slot, send, recv, stop, stop_send, stop_recv, number):
        self.place = place
        self.low, self.high = pair(rim.at[0]), pair(rim.at[1])
        stop = stop.at[number]

        def copy(src, dst, send_sem, recv_sem, device):
            return pltpu.make_async_remote_copy(
                src_ref=src,
                dst_ref=dst,
                send_sem=send_sem,
                recv_sem=recv_sem,
                device_id=device,
                device_id_type=MESH,
            )

        last = place.group - 1
        self.direct, self.split, self.onward = [], [], []
        for side, (target, step, edge, other, onward) in enumerate(
            (
                (self.low, 1, place.at_end, place.in_group(0), place.in_group(place.group)),
                (self.high, -1, place.at_start, place.in_group(last), place.in_group(-1)),
            )
        ):
            near = place.beside("col", step)
            here = slot + 2 * side
            self.direct.append(copy(source[0], target[0], send.at[here], recv.at[here], near))
            here += 1
            plain = copy(source[1], target[1], send.at[here], recv.at[here], near)
            turned = copy(source[1], stop, send.at[here], stop_recv.at[number], other)
            self.split.append((edge, plain, turned))
            relay = place.at_start if side == 0 else place.at_end
            self.onward.append(
                (relay, turned, copy(stop, target[1], stop_send.at[number], recv.at[here], onward))
            )

    def start_split(self):
        for edge, plain, turned in self.split:

            @pl.when(edge)
            def _():
                turned.start()

            @pl.when(jnp.logical_not(edge))
            def _():
                plain.start()

    def start_direct(self):
        for copy in self.direct:
            copy.start()

    def relay(self):
        for edge, turned, onward in self.onward:

            @pl.when(edge)
            def _():
                turned.wait_recv()
                onward.start()

    def wait_low(self):
        self.direct[0].wait_recv()
        self.split[0][1].wait_recv()

    def wait_high(self):
        self.direct[1].wait_recv()
        self.split[1][1].wait_recv()

    def wait_send(self):
        for copy in self.direct:
            copy.wait_send()
        for _, plain, _ in self.split:
            plain.wait_send()
        for edge, _, onward in self.onward:

            @pl.when(edge)
            def _():
                onward.wait_send()


def put(field, total, pick):
    for angle in range(2):
        for part in range(2):
            field[angle][part] = pick(total, angle, part).astype(jnp.bfloat16)


def first(rows, cols, *refs):
    order, band, tilt, shift, obj_hbm, bank_hbm, cot_hbm = refs[:7]
    u_0, u_1, q_0, q_1, psi_out = refs[7:12]
    mine, rim, stop, send, recv, stop_send, stop_recv, obj, bank, cot, load = refs[12:]
    odd = [shift[angle, 0] % 2 == 1 for angle in range(2)]
    u_out, q_out = (u_0, u_1), (q_0, q_1)
    place = Place(rows, cols)
    place.greet()
    loads = [
        pltpu.make_async_copy(source, target, load.at[number])
        for number, (source, target) in enumerate(
            ((obj_hbm, obj), (cot_hbm, cot), (bank_hbm, bank))
        )
    ]
    for copy in loads:
        copy.start()
    width = bank.shape[2]
    here, later = order[0], order[1]
    fields = incident(tilt, place.row * width, place.col * width, rows * width, width)
    u_mine, v_mine, h_mine = pair(mine.at[0]), pair(mine.at[1]), pair(mine.at[2])
    g_mine = pair(cot)
    loads[0].wait()
    t_real, t_imag = obj[here, 0], obj[here, 1]
    for angle in range(2):
        real = fields[angle][0].astype(jnp.float32)
        imag = fields[angle][1].astype(jnp.float32)
        u_mine[angle][0] = (t_real * real - t_imag * imag).astype(jnp.bfloat16)
        u_mine[angle][1] = (t_real * imag + t_imag * real).astype(jnp.bfloat16)
    loads[1].wait()
    place.met()
    relays = (stop, stop_send, stop_recv)
    halo_u = Rows(place, (mine.at[0],), (rim.at[0], rim.at[1]), (1, -1), 0, send, recv)
    halo_g = Cols(place, g_mine, rim.at[pl.ds(2, 2)], 4, send, recv, *relays, 0)
    halo_v = Cols(place, v_mine, rim.at[pl.ds(4, 2)], 8, send, recv, *relays, 1)
    halo_h = Rows(place, (mine.at[2],), (rim.at[6], rim.at[7], rim.at[8]), (1, -1, -2), 12, send, recv)
    halo_g.start_split()
    halo_u.start()
    halo_g.start_direct()
    loads[2].wait()
    v = row_term(left_matrix(bank, band[0, 0, 1]), u_mine)
    h = col_adjoint_term(g_mine, right_matrix(bank, band[1, 1, 1]))
    halo_g.relay()
    halo_u.wait(0)
    v += row_term(left_matrix(bank, band[0, 0, 0]), halo_u.got[0])
    halo_u.wait(1)
    v += row_term(left_matrix(bank, band[0, 0, 2]), halo_u.got[1])
    put(v_mine, v, from_component)
    halo_v.start_split()
    halo_v.start_direct()
    p = col_term(v_mine, right_matrix(bank, band[0, 1, 1]))
    halo_v.relay()
    halo_g.wait_low()
    h += col_adjoint_term(halo_g.low, right_matrix(bank, band[1, 1, 2]))
    halo_g.wait_high()
    h += col_adjoint_term(halo_g.high, right_matrix(bank, band[1, 1, 0]))
    put(h_mine, h, from_angle)
    halo_h.start()
    halo_h.wait(1)
    middle = choose(odd, halo_h.got[1], h_mine)
    q = row_term(left_adjoint(bank, band[1, 0, 1]), middle)
    halo_h.wait(0)
    q += row_term(left_adjoint(bank, band[1, 0, 2]), choose(odd, h_mine, halo_h.got[0]))
    halo_h.wait(2)
    q += row_term(left_adjoint(bank, band[1, 0, 0]), choose(odd, halo_h.got[2], halo_h.got[1]))
    put(q_out, q, from_component)
    halo_v.wait_low()
    p += col_term(halo_v.low, right_matrix(bank, band[0, 1, 0]))
    halo_v.wait_high()
    p += col_term(halo_v.high, right_matrix(bank, band[0, 1, 2]))
    s_real, s_imag = obj[later, 0], obj[later, 1]
    for angle in range(2):
        real = from_angle(p, angle, 0).astype(jnp.bfloat16)
        imag = from_angle(p, angle, 1).astype(jnp.bfloat16)
        psi_out[angle, 0] = real
        psi_out[angle, 1] = imag
        real, imag = real.astype(jnp.float32), imag.astype(jnp.float32)
        u_out[angle][0] = (s_real * real - s_imag * imag).astype(jnp.bfloat16)
        u_out[angle][1] = (s_real * imag + s_imag * real).astype(jnp.bfloat16)
    for halo in (halo_u, halo_g, halo_v, halo_h):
        halo.wait_send()


def second(rows, cols, *refs):
    order, band, tilt, shift, obj, bank, u_0, u_1, q_0, q_1, psi, exit_out, grad_out = refs[:13]
    mine, rim, stop, send, recv, stop_send, stop_recv = refs[13:]
    odd = [shift[angle, 0] % 2 == 1 for angle in range(2)]
    u, q = (u_0, u_1), (q_0, q_1)
    place = Place(rows, cols)
    place.greet()
    width = bank.shape[2]
    later = order[1]
    g_mine, v_mine, h_mine = pair(mine.at[0]), pair(mine.at[1]), pair(mine.at[2])
    s_real, s_imag = obj[later, 0], obj[later, 1]
    last_real = None
    last_imag = None
    for angle in range(2):
        q_real, q_imag = q[angle][0].astype(jnp.float32), q[angle][1].astype(jnp.float32)
        g_mine[angle][0] = (q_real * s_real + q_imag * s_imag).astype(jnp.bfloat16)
        g_mine[angle][1] = (q_imag * s_real - q_real * s_imag).astype(jnp.bfloat16)
        real, imag = psi[angle, 0].astype(jnp.float32), psi[angle, 1].astype(jnp.float32)
        add_real = q_real * real + q_imag * imag
        add_imag = q_imag * real - q_real * imag
        last_real = add_real if last_real is None else last_real + add_real
        last_imag = add_imag if last_imag is None else last_imag + add_imag
    place.met()
    relays = (stop, stop_send, stop_recv)
    halo_u = Rows(place, u, (rim.at[0], rim.at[1], rim.at[8]), (1, -1, 2), 12, send, recv)
    halo_g = Cols(place, g_mine, rim.at[pl.ds(2, 2)], 4, send, recv, *relays, 0)
    halo_v = Cols(place, v_mine, rim.at[pl.ds(4, 2)], 8, send, recv, *relays, 1)
    halo_h = Rows(place, (mine.at[2],), (rim.at[6], rim.at[7]), (1, -1), 0, send, recv)
    halo_g.start_split()
    halo_u.start()
    halo_g.start_direct()
    h = col_adjoint_term(g_mine, right_matrix(bank, band[0, 1, 1]))
    halo_g.relay()
    halo_u.wait(0)
    v = row_term(left_matrix(bank, band[1, 0, 1]), choose(odd, halo_u.got[0], u))
    halo_u.wait(1)
    v += row_term(left_matrix(bank, band[1, 0, 2]), choose(odd, u, halo_u.got[1]))
    halo_u.wait(2)
    v += row_term(left_matrix(bank, band[1, 0, 0]), choose(odd, halo_u.got[2], halo_u.got[0]))
    put(v_mine, v, from_component)
    halo_v.start_split()
    halo_v.start_direct()
    p = col_term(v_mine, right_matrix(bank, band[1, 1, 1]))
    halo_v.relay()
    halo_g.wait_low()
    h += col_adjoint_term(halo_g.low, right_matrix(bank, band[0, 1, 2]))
    halo_g.wait_high()
    h += col_adjoint_term(halo_g.high, right_matrix(bank, band[0, 1, 0]))
    put(h_mine, h, from_angle)
    halo_h.start()
    fields = incident(tilt, place.row * width, place.col * width, rows * width, width)
    b = row_term(left_adjoint(bank, band[0, 0, 1]), h_mine)
    halo_h.wait(0)
    b += row_term(left_adjoint(bank, band[0, 0, 2]), halo_h.got[0])
    halo_h.wait(1)
    b += row_term(left_adjoint(bank, band[0, 0, 0]), halo_h.got[1])
    first_real = None
    first_imag = None
    for angle in range(2):
        q_real = from_component(b, angle, 0).astype(jnp.bfloat16).astype(jnp.float32)
        q_imag = from_component(b, angle, 1).astype(jnp.bfloat16).astype(jnp.float32)
        real, imag = fields[angle][0].astype(jnp.float32), fields[angle][1].astype(jnp.float32)
        add_real = q_real * real + q_imag * imag
        add_imag = q_imag * real - q_real * imag
        first_real = add_real if first_real is None else first_real + add_real
        first_imag = add_imag if first_imag is None else first_imag + add_imag
    swapped = later == 0
    grad_out[0, 0] = jnp.where(swapped, last_real, first_real)
    grad_out[0, 1] = jnp.where(swapped, last_imag, first_imag)
    grad_out[1, 0] = jnp.where(swapped, first_real, last_real)
    grad_out[1, 1] = jnp.where(swapped, first_imag, last_imag)
    halo_v.wait_low()
    p += col_term(halo_v.low, right_matrix(bank, band[1, 1, 0]))
    halo_v.wait_high()
    p += col_term(halo_v.high, right_matrix(bank, band[1, 1, 2]))
    put(pair(exit_out), p, from_angle)
    for halo in (halo_u, halo_g, halo_v, halo_h):
        halo.wait_send()


def call(body, outs, arrays, held, number, limit):
    width = held[0].shape[2]
    field = (2, 2, width, width)
    smem = pl.BlockSpec(memory_space=pltpu.SMEM)
    vmem = pl.BlockSpec(memory_space=pltpu.VMEM)
    specs = [smem] * 4 + [vmem] * (len(arrays) - 4)
    extra = []
    if len(held) == 3:
        specs = [smem] * 4 + [pl.BlockSpec(memory_space=pltpu.HBM)] * 3
        extra = [pltpu.VMEM(array.shape, array.dtype) for array in arrays[4:]]
        extra.append(pltpu.SemaphoreType.DMA((3,)))
    return pl.pallas_call(
        body,
        out_shape=outs,
        in_specs=specs,
        out_specs=[vmem] * len(outs),
        scratch_shapes=[
            pltpu.VMEM((3, *field), jnp.bfloat16),
            pltpu.VMEM((9, *field), jnp.bfloat16),
            pltpu.VMEM((2, *field[1:]), jnp.bfloat16),
            pltpu.SemaphoreType.DMA((18,)),
            pltpu.SemaphoreType.DMA((18,)),
            pltpu.SemaphoreType.DMA((2,)),
            pltpu.SemaphoreType.DMA((2,)),
            *extra,
        ],
        compiler_params=pltpu.CompilerParams(
            collective_id=number, has_side_effects=True, vmem_limit_bytes=limit
        ),
    )(*arrays)


def swap(row_step, col_step, rows, cols, u, q, u_out, q_out, send, recv):
    row, col = lax.axis_index("row"), lax.axis_index("col")
    ahead = (lax.rem(row + row_step, rows), lax.rem(col + col_step, cols))
    behind = (lax.rem(row + -row_step % rows, rows), lax.rem(col + -col_step % cols, cols))
    barrier = pltpu.get_barrier_semaphore()
    for other in (ahead, behind):
        pl.semaphore_signal(barrier, inc=1, device_id=other, device_id_type=MESH)
    pl.semaphore_wait(barrier, 2)
    copies = [
        pltpu.make_async_remote_copy(
            src_ref=source,
            dst_ref=target,
            send_sem=send.at[slot],
            recv_sem=recv.at[slot],
            device_id=other,
            device_id_type=MESH,
        )
        for slot, (source, target, other) in enumerate(((u, u_out, ahead), (q, q_out, behind)))
    ]
    for copy in copies:
        copy.start()
    for copy in copies:
        copy.wait()


def move(row_step, col_step, rows, cols, u, q):
    if row_step == 0 and col_step == 0:
        return u, q
    vmem = pl.BlockSpec(memory_space=pltpu.VMEM)
    return pl.pallas_call(
        functools.partial(swap, row_step, col_step, rows, cols),
        out_shape=[jax.ShapeDtypeStruct(u.shape, u.dtype)] * 2,
        in_specs=[vmem] * 2,
        out_specs=[vmem] * 2,
        scratch_shapes=[pltpu.SemaphoreType.DMA((2,)), pltpu.SemaphoreType.DMA((2,))],
        compiler_params=pltpu.CompilerParams(
            collective_id=1 + row_step // 2 * SHIFTS + col_step,
            has_side_effects=True,
            vmem_limit_bytes=VMEM_LIMIT,
        ),
    )(u, q)


def local(rows, cols, obj, bank, band_index, tilt, tile_shift, slice_order, cot):
    field = jax.ShapeDtypeStruct(cot.shape, jnp.bfloat16)
    part = jax.ShapeDtypeStruct(cot.shape[1:], jnp.bfloat16)
    u_0, u_1, q_0, q_1, psi = call(
        functools.partial(first, rows, cols),
        (part, part, part, part, field),
        (slice_order, band_index, tilt, tile_shift, obj, bank, cot),
        (bank, obj, cot),
        0,
        FIRST_LIMIT,
    )
    weight = jnp.array([SHIFTS, 1], jnp.int32)
    choice = [
        jnp.sum((shift >> jnp.array([1, 0], jnp.int32)) * weight)
        for shift in (tile_shift[0], lax.optimization_barrier(tile_shift)[1])
    ]
    branches = [
        functools.partial(move, row_step, col_step, rows, cols)
        for row_step in range(0, SHIFTS, 2)
        for col_step in range(SHIFTS)
    ]
    branches = tuple(jax.make_jaxpr(branch)(u_0, q_0) for branch in branches)
    u_0, q_0 = cond_p.bind(choice[0], u_0, q_0, branches=branches)
    u_1, q_1 = cond_p.bind(choice[1], u_1, q_1, branches=branches)
    exit_field, grad = call(
        functools.partial(second, rows, cols),
        (field, jax.ShapeDtypeStruct(obj.shape, jnp.float32)),
        (slice_order, band_index, tilt, tile_shift, obj, bank, u_0, u_1, q_0, q_1, psi),
        (bank,),
        1,
        VMEM_LIMIT,
    )
    return exit_field, grad


def solution(mesh):
    field = P(None, None, "row", "col")
    return jax.shard_map(
        functools.partial(local, mesh.shape["row"], mesh.shape["col"]),
        mesh=mesh,
        in_specs=(field, P(), P(), P(), P(), P(), field),
        out_specs=(field, field),
        check_vma=False,
    )
```

```python
import functools
import math

import jax
import jax.numpy as jnp
from jax import lax
from jax.extend.core.primitives import cond_p
from jax.experimental import pallas as pl
from jax.experimental.pallas import tpu as pltpu
from jax.sharding import PartitionSpec as P

MESH = pl.DeviceIdType.MESH
SHIFTS = 8
GROUP = 8
VMEM_LIMIT = 16 << 20
FIRST_LIMIT = 61 << 20


def left_matrix(bank, index):
    real, imag = bank[index, 0], bank[index, 1]
    return jnp.concatenate(
        [jnp.concatenate([real, -imag], axis=1), jnp.concatenate([imag, real], axis=1)], axis=0
    )


def left_adjoint(bank, index):
    real = bank[index, 0].astype(jnp.float32).T.astype(jnp.bfloat16)
    imag = bank[index, 1].astype(jnp.float32).T.astype(jnp.bfloat16)
    return jnp.concatenate(
        [jnp.concatenate([real, imag], axis=1), jnp.concatenate([-imag, real], axis=1)], axis=0
    )


def right_matrix(bank, index):
    real, imag = bank[index, 0], bank[index, 1]
    return jnp.concatenate(
        [jnp.concatenate([real, imag], axis=1), jnp.concatenate([-imag, real], axis=1)], axis=0
    )


def by_component(field):
    return jnp.concatenate(
        [
            jnp.concatenate([field[0][0], field[1][0]], axis=1),
            jnp.concatenate([field[0][1], field[1][1]], axis=1),
        ],
        axis=0,
    )


def by_angle(field):
    return jnp.concatenate(
        [
            jnp.concatenate([field[0][0], field[0][1]], axis=1),
            jnp.concatenate([field[1][0], field[1][1]], axis=1),
        ],
        axis=0,
    )


def row_term(matrix, field):
    return jnp.dot(matrix, by_component(field), preferred_element_type=jnp.float32)


def col_term(field, matrix):
    return jnp.dot(by_angle(field), matrix, preferred_element_type=jnp.float32)


def col_adjoint_term(field, matrix):
    return lax.dot_general(
        by_angle(field), matrix, (((1,), (1,)), ((), ())), preferred_element_type=jnp.float32
    )


def from_component(total, angle, part):
    n = total.shape[0] // 2
    return total[part * n : (part + 1) * n, angle * n : (angle + 1) * n]


def from_angle(total, angle, part):
    n = total.shape[0] // 2
    return total[angle * n : (angle + 1) * n, part * n : (part + 1) * n]


def incident(tilt, row_start, col_start, period, width):
    line = lax.broadcasted_iota(jnp.int32, (8, width), 0)
    spot = lax.broadcasted_iota(jnp.int32, (8, width), 1)
    rate = jnp.where(
        line == 0,
        tilt[0, 0],
        jnp.where(line == 1, tilt[0, 1], jnp.where(line == 2, tilt[1, 0], tilt[1, 1])),
    )
    start = jnp.where(line % 2 == 0, row_start, col_start)
    turns = (rate * (start + spot)) & (period - 1)
    phase = turns.astype(jnp.float32) * (2.0 * math.pi / period)
    cos, sin = jnp.cos(phase), jnp.sin(phase)
    cos_t, sin_t = cos.T, sin.T
    fields = []
    for angle in range(2):
        row_cos = cos_t[:, 2 * angle : 2 * angle + 1]
        row_sin = sin_t[:, 2 * angle : 2 * angle + 1]
        col_cos = cos[2 * angle + 1 : 2 * angle + 2, :]
        col_sin = sin[2 * angle + 1 : 2 * angle + 2, :]
        fields.append(
            (
                (row_cos * col_cos - row_sin * col_sin).astype(jnp.bfloat16),
                (row_sin * col_cos + row_cos * col_sin).astype(jnp.bfloat16),
            )
        )
    return fields


def pair(ref):
    return ref.at[0], ref.at[1]


class Place:
    def __init__(self, rows, cols):
        self.rows, self.cols = rows, cols
        self.group = min(GROUP, cols // 2)
        self.row, self.col = lax.axis_index("row"), lax.axis_index("col")
        self.spot = lax.rem(self.col, self.group)
        self.base = self.col - self.spot
        self.at_start = self.spot == 0
        self.at_end = self.spot == self.group - 1

    def beside(self, axis, step):
        if axis == "row":
            return lax.rem(self.row + self.rows + step, self.rows), self.col
        return self.row, lax.rem(self.col + self.cols + step, self.cols)

    def in_group(self, step):
        return self.row, lax.rem(self.base + self.cols + step, self.cols)

    def greet(self):
        barrier = pltpu.get_barrier_semaphore()

        def hail(device):
            pl.semaphore_signal(barrier, inc=1, device_id=device, device_id_type=MESH)

        for axis, step in (("row", 1), ("row", -1), ("row", 2), ("row", -2), ("col", 1), ("col", -1)):
            hail(self.beside(axis, step))

        @pl.when(self.at_start)
        def _():
            hail(self.in_group(self.group - 1))

        @pl.when(self.at_end)
        def _():
            hail(self.in_group(0))

    def met(self):
        edge = (self.at_start | self.at_end).astype(jnp.int32)
        pl.semaphore_wait(pltpu.get_barrier_semaphore(), 6 + edge)


class Rows:
    def __init__(self, place, sources, rims, steps, slot, send, recv):
        self.got = [pair(rim) for rim in rims]
        self.each = len(sources)
        self.copies = []
        for rim, step in zip(rims, steps):
            for part, source in enumerate(sources):
                here = slot + len(self.copies)
                self.copies.append(
                    pltpu.make_async_remote_copy(
                        src_ref=source,
                        dst_ref=rim if self.each == 1 else rim.at[part],
                        send_sem=send.at[here],
                        recv_sem=recv.at[here],
                        device_id=place.beside("row", step),
                        device_id_type=MESH,
                    )
                )

    def start(self):
        for copy in self.copies:
            copy.start()

    def wait(self, side):
        for copy in self.copies[side * self.each : (side + 1) * self.each]:
            copy.wait_recv()

    def wait_send(self):
        for copy in self.copies:
            copy.wait_send()


def choose(odd, moved, still):
    return [
        [jnp.where(odd[angle], moved[angle][part], still[angle][part]) for part in range(2)]
        for angle in range(2)
    ]


class Cols:
    def __init__(self, place, source, rim, slot, send, recv, stop, stop_send, stop_recv, number):
        self.place = place
        self.low, self.high = pair(rim.at[0]), pair(rim.at[1])
        stop = stop.at[number]

        def copy(src, dst, send_sem, recv_sem, device):
            return pltpu.make_async_remote_copy(
                src_ref=src,
                dst_ref=dst,
                send_sem=send_sem,
                recv_sem=recv_sem,
                device_id=device,
                device_id_type=MESH,
            )

        last = place.group - 1
        self.direct, self.split, self.onward = [], [], []
        for side, (target, step, edge, other, onward) in enumerate(
            (
                (self.low, 1, place.at_end, place.in_group(0), place.in_group(place.group)),
                (self.high, -1, place.at_start, place.in_group(last), place.in_group(-1)),
            )
        ):
            near = place.beside("col", step)
            here = slot + 2 * side
            self.direct.append(copy(source[0], target[0], send.at[here], recv.at[here], near))
            here += 1
            plain = copy(source[1], target[1], send.at[here], recv.at[here], near)
            turned = copy(source[1], stop, send.at[here], stop_recv.at[number], other)
            self.split.append((edge, plain, turned))
            relay = place.at_start if side == 0 else place.at_end
            self.onward.append(
                (relay, turned, copy(stop, target[1], stop_send.at[number], recv.at[here], onward))
            )

    def start_split(self):
        for edge, plain, turned in self.split:

            @pl.when(edge)
            def _():
                turned.start()

            @pl.when(jnp.logical_not(edge))
            def _():
                plain.start()

    def start_direct(self):
        for copy in self.direct:
            copy.start()

    def relay(self):
        for edge, turned, onward in self.onward:

            @pl.when(edge)
            def _():
                turned.wait_recv()
                onward.start()

    def wait_low(self):
        self.direct[0].wait_recv()
        self.split[0][1].wait_recv()

    def wait_high(self):
        self.direct[1].wait_recv()
        self.split[1][1].wait_recv()

    def wait_send(self):
        for copy in self.direct:
            copy.wait_send()
        for _, plain, _ in self.split:
            plain.wait_send()
        for edge, _, onward in self.onward:

            @pl.when(edge)
            def _():
                onward.wait_send()


def put(field, total, pick):
    for angle in range(2):
        for part in range(2):
            field[angle][part] = pick(total, angle, part).astype(jnp.bfloat16)


def first(rows, cols, *refs):
    order, band, tilt, shift, obj_hbm, bank_hbm, cot_hbm = refs[:7]
    u_0, u_1, q_0, q_1, psi_out = refs[7:12]
    mine, rim, stop, send, recv, stop_send, stop_recv, obj, bank, cot, load = refs[12:]
    odd = [shift[angle, 0] % 2 == 1 for angle in range(2)]
    u_out, q_out = (u_0, u_1), (q_0, q_1)
    place = Place(rows, cols)
    place.greet()
    loads = [
        pltpu.make_async_copy(source, target, load.at[number])
        for number, (source, target) in enumerate(
            ((obj_hbm, obj), (cot_hbm, cot), (bank_hbm, bank))
        )
    ]
    for copy in loads:
        copy.start()
    width = bank.shape[2]
    here, later = order[0], order[1]
    fields = incident(tilt, place.row * width, place.col * width, rows * width, width)
    u_mine, v_mine, h_mine = pair(mine.at[0]), pair(mine.at[1]), pair(mine.at[2])
    g_mine = pair(cot)
    loads[0].wait()
    t_real, t_imag = obj[here, 0], obj[here, 1]
    for angle in range(2):
        real = fields[angle][0].astype(jnp.float32)
        imag = fields[angle][1].astype(jnp.float32)
        u_mine[angle][0] = (t_real * real - t_imag * imag).astype(jnp.bfloat16)
        u_mine[angle][1] = (t_real * imag + t_imag * real).astype(jnp.bfloat16)
    loads[1].wait()
    place.met()
    relays = (stop, stop_send, stop_recv)
    halo_u = Rows(place, (mine.at[0],), (rim.at[0], rim.at[1]), (1, -1), 0, send, recv)
    halo_g = Cols(place, g_mine, rim.at[pl.ds(2, 2)], 4, send, recv, *relays, 0)
    halo_v = Cols(place, v_mine, rim.at[pl.ds(4, 2)], 8, send, recv, *relays, 1)
    halo_h = Rows(place, (mine.at[2],), (rim.at[6], rim.at[7], rim.at[8]), (1, -1, -2), 12, send, recv)
    halo_g.start_split()
    halo_u.start()
    halo_g.start_direct()
    loads[2].wait()
    v = row_term(left_matrix(bank, band[0, 0, 1]), u_mine)
    h = col_adjoint_term(g_mine, right_matrix(bank, band[1, 1, 1]))
    halo_g.relay()
    halo_u.wait(0)
    v += row_term(left_matrix(bank, band[0, 0, 0]), halo_u.got[0])
    halo_u.wait(1)
    v += row_term(left_matrix(bank, band[0, 0, 2]), halo_u.got[1])
    put(v_mine, v, from_component)
    halo_v.start_split()
    halo_v.start_direct()
    p = col_term(v_mine, right_matrix(bank, band[0, 1, 1]))
    halo_v.relay()
    halo_g.wait_low()
    h += col_adjoint_term(halo_g.low, right_matrix(bank, band[1, 1, 2]))
    halo_g.wait_high()
    h += col_adjoint_term(halo_g.high, right_matrix(bank, band[1, 1, 0]))
    put(h_mine, h, from_angle)
    halo_h.start()
    halo_h.wait(1)
    middle = choose(odd, halo_h.got[1], h_mine)
    q = row_term(left_adjoint(bank, band[1, 0, 1]), middle)
    halo_h.wait(0)
    q += row_term(left_adjoint(bank, band[1, 0, 2]), choose(odd, h_mine, halo_h.got[0]))
    halo_h.wait(2)
    q += row_term(left_adjoint(bank, band[1, 0, 0]), choose(odd, halo_h.got[2], halo_h.got[1]))
    put(q_out, q, from_component)
    halo_v.wait_low()
    p += col_term(halo_v.low, right_matrix(bank, band[0, 1, 0]))
    halo_v.wait_high()
    p += col_term(halo_v.high, right_matrix(bank, band[0, 1, 2]))
    s_real, s_imag = obj[later, 0], obj[later, 1]
    for angle in range(2):
        real = from_angle(p, angle, 0).astype(jnp.bfloat16)
        imag = from_angle(p, angle, 1).astype(jnp.bfloat16)
        psi_out[angle, 0] = real
        psi_out[angle, 1] = imag
        real, imag = real.astype(jnp.float32), imag.astype(jnp.float32)
        u_out[angle][0] = (s_real * real - s_imag * imag).astype(jnp.bfloat16)
        u_out[angle][1] = (s_real * imag + s_imag * real).astype(jnp.bfloat16)
    for halo in (halo_u, halo_g, halo_v, halo_h):
        halo.wait_send()


def second(rows, cols, *refs):
    order, band, tilt, shift, obj, bank, u_0, u_1, q_0, q_1, psi, exit_out, grad_out = refs[:13]
    mine, rim, stop, send, recv, stop_send, stop_recv = refs[13:]
    odd = [shift[angle, 0] % 2 == 1 for angle in range(2)]
    u, q = (u_0, u_1), (q_0, q_1)
    place = Place(rows, cols)
    place.greet()
    width = bank.shape[2]
    later = order[1]
    g_mine, v_mine, h_mine = pair(mine.at[0]), pair(mine.at[1]), pair(mine.at[2])
    s_real, s_imag = obj[later, 0], obj[later, 1]
    last_real = None
    last_imag = None
    for angle in range(2):
        q_real, q_imag = q[angle][0].astype(jnp.float32), q[angle][1].astype(jnp.float32)
        g_mine[angle][0] = (q_real * s_real + q_imag * s_imag).astype(jnp.bfloat16)
        g_mine[angle][1] = (q_imag * s_real - q_real * s_imag).astype(jnp.bfloat16)
        real, imag = psi[angle, 0].astype(jnp.float32), psi[angle, 1].astype(jnp.float32)
        add_real = q_real * real + q_imag * imag
        add_imag = q_imag * real - q_real * imag
        last_real = add_real if last_real is None else last_real + add_real
        last_imag = add_imag if last_imag is None else last_imag + add_imag
    place.met()
    relays = (stop, stop_send, stop_recv)
    halo_u = Rows(place, u, (rim.at[0], rim.at[1], rim.at[8]), (1, -1, 2), 12, send, recv)
    halo_g = Cols(place, g_mine, rim.at[pl.ds(2, 2)], 4, send, recv, *relays, 0)
    halo_v = Cols(place, v_mine, rim.at[pl.ds(4, 2)], 8, send, recv, *relays, 1)
    halo_h = Rows(place, (mine.at[2],), (rim.at[6], rim.at[7]), (1, -1), 0, send, recv)
    halo_g.start_split()
    halo_u.start()
    halo_g.start_direct()
    h = col_adjoint_term(g_mine, right_matrix(bank, band[0, 1, 1]))
    halo_g.relay()
    halo_u.wait(0)
    v = row_term(left_matrix(bank, band[1, 0, 1]), choose(odd, halo_u.got[0], u))
    halo_u.wait(1)
    v += row_term(left_matrix(bank, band[1, 0, 2]), choose(odd, u, halo_u.got[1]))
    halo_u.wait(2)
    v += row_term(left_matrix(bank, band[1, 0, 0]), choose(odd, halo_u.got[2], halo_u.got[0]))
    put(v_mine, v, from_component)
    halo_v.start_split()
    halo_v.start_direct()
    p = col_term(v_mine, right_matrix(bank, band[1, 1, 1]))
    halo_v.relay()
    halo_g.wait_low()
    h += col_adjoint_term(halo_g.low, right_matrix(bank, band[0, 1, 2]))
    halo_g.wait_high()
    h += col_adjoint_term(halo_g.high, right_matrix(bank, band[0, 1, 0]))
    put(h_mine, h, from_angle)
    halo_h.start()
    fields = incident(tilt, place.row * width, place.col * width, rows * width, width)
    b = row_term(left_adjoint(bank, band[0, 0, 1]), h_mine)
    halo_h.wait(0)
    b += row_term(left_adjoint(bank, band[0, 0, 2]), halo_h.got[0])
    halo_h.wait(1)
    b += row_term(left_adjoint(bank, band[0, 0, 0]), halo_h.got[1])
    first_real = None
    first_imag = None
    for angle in range(2):
        q_real = from_component(b, angle, 0).astype(jnp.bfloat16).astype(jnp.float32)
        q_imag = from_component(b, angle, 1).astype(jnp.bfloat16).astype(jnp.float32)
        real, imag = fields[angle][0].astype(jnp.float32), fields[angle][1].astype(jnp.float32)
        add_real = q_real * real + q_imag * imag
        add_imag = q_imag * real - q_real * imag
        first_real = add_real if first_real is None else first_real + add_real
        first_imag = add_imag if first_imag is None else first_imag + add_imag
    swapped = later == 0
    grad_out[0, 0] = jnp.where(swapped, last_real, first_real)
    grad_out[0, 1] = jnp.where(swapped, last_imag, first_imag)
    grad_out[1, 0] = jnp.where(swapped, first_real, last_real)
    grad_out[1, 1] = jnp.where(swapped, first_imag, last_imag)
    halo_v.wait_low()
    p += col_term(halo_v.low, right_matrix(bank, band[1, 1, 0]))
    halo_v.wait_high()
    p += col_term(halo_v.high, right_matrix(bank, band[1, 1, 2]))
    put(pair(exit_out), p, from_angle)
    for halo in (halo_u, halo_g, halo_v, halo_h):
        halo.wait_send()


def call(body, outs, arrays, held, number, limit):
    width = held[0].shape[2]
    field = (2, 2, width, width)
    smem = pl.BlockSpec(memory_space=pltpu.SMEM)
    vmem = pl.BlockSpec(memory_space=pltpu.VMEM)
    specs = [smem] * 4 + [vmem] * (len(arrays) - 4)
    extra = []
    if len(held) == 3:
        specs = [smem] * 4 + [pl.BlockSpec(memory_space=pltpu.HBM)] * 3
        extra = [pltpu.VMEM(array.shape, array.dtype) for array in arrays[4:]]
        extra.append(pltpu.SemaphoreType.DMA((3,)))
    return pl.pallas_call(
        body,
        out_shape=outs,
        in_specs=specs,
        out_specs=[vmem] * len(outs),
        scratch_shapes=[
            pltpu.VMEM((3, *field), jnp.bfloat16),
            pltpu.VMEM((9, *field), jnp.bfloat16),
            pltpu.VMEM((2, *field[1:]), jnp.bfloat16),
            pltpu.SemaphoreType.DMA((18,)),
            pltpu.SemaphoreType.DMA((18,)),
            pltpu.SemaphoreType.DMA((2,)),
            pltpu.SemaphoreType.DMA((2,)),
            *extra,
        ],
        compiler_params=pltpu.CompilerParams(
            collective_id=number, has_side_effects=True, vmem_limit_bytes=limit
        ),
    )(*arrays)


def swap(row_step, col_step, rows, cols, u, q, u_out, q_out, send, recv):
    row, col = lax.axis_index("row"), lax.axis_index("col")
    ahead = (lax.rem(row + row_step, rows), lax.rem(col + col_step, cols))
    behind = (lax.rem(row + -row_step % rows, rows), lax.rem(col + -col_step % cols, cols))
    barrier = pltpu.get_barrier_semaphore()
    for other in (ahead, behind):
        pl.semaphore_signal(barrier, inc=1, device_id=other, device_id_type=MESH)
    pl.semaphore_wait(barrier, 2)
    copies = [
        pltpu.make_async_remote_copy(
            src_ref=source,
            dst_ref=target,
            send_sem=send.at[slot],
            recv_sem=recv.at[slot],
            device_id=other,
            device_id_type=MESH,
        )
        for slot, (source, target, other) in enumerate(((u, u_out, ahead), (q, q_out, behind)))
    ]
    for copy in copies:
        copy.start()
    for copy in copies:
        copy.wait()


def move(row_step, col_step, rows, cols, u, q):
    if row_step == 0 and col_step == 0:
        return u, q
    vmem = pl.BlockSpec(memory_space=pltpu.VMEM)
    return pl.pallas_call(
        functools.partial(swap, row_step, col_step, rows, cols),
        out_shape=[jax.ShapeDtypeStruct(u.shape, u.dtype)] * 2,
        in_specs=[vmem] * 2,
        out_specs=[vmem] * 2,
        scratch_shapes=[pltpu.SemaphoreType.DMA((2,)), pltpu.SemaphoreType.DMA((2,))],
        compiler_params=pltpu.CompilerParams(
            collective_id=1 + row_step // 2 * SHIFTS + col_step,
            has_side_effects=True,
            vmem_limit_bytes=VMEM_LIMIT,
        ),
    )(u, q)


def local(rows, cols, obj, bank, band_index, tilt, tile_shift, slice_order, cot):
    field = jax.ShapeDtypeStruct(cot.shape, jnp.bfloat16)
    part = jax.ShapeDtypeStruct(cot.shape[1:], jnp.bfloat16)
    u_0, u_1, q_0, q_1, psi = call(
        functools.partial(first, rows, cols),
        (part, part, part, part, field),
        (slice_order, band_index, tilt, tile_shift, obj, bank, cot),
        (bank, obj, cot),
        0,
        FIRST_LIMIT,
    )
    choice = [
        jnp.sum(jnp.where(lax.iota(jnp.int32, 2) == 0, (shift >> 1) * SHIFTS, shift))
        for shift in (tile_shift[0], lax.optimization_barrier(tile_shift)[1])
    ]
    branches = [
        functools.partial(move, row_step, col_step, rows, cols)
        for row_step in range(0, SHIFTS, 2)
        for col_step in range(SHIFTS)
    ]
    branches = tuple(jax.make_jaxpr(branch)(u_0, q_0) for branch in branches)
    u_0, q_0 = cond_p.bind(choice[0], u_0, q_0, branches=branches)
    u_1, q_1 = cond_p.bind(choice[1], u_1, q_1, branches=branches)
    exit_field, grad = call(
        functools.partial(second, rows, cols),
        (field, jax.ShapeDtypeStruct(obj.shape, jnp.float32)),
        (slice_order, band_index, tilt, tile_shift, obj, bank, u_0, u_1, q_0, q_1, psi),
        (bank,),
        1,
        VMEM_LIMIT,
    )
    return exit_field, grad


def solution(mesh):
    field = P(None, None, "row", "col")
    return jax.shard_map(
        functools.partial(local, mesh.shape["row"], mesh.shape["col"]),
        mesh=mesh,
        in_specs=(field, P(), P(), P(), P(), P(), field),
        out_specs=(field, field),
        check_vma=False,
    )
```
